32 devices in a mesh: shard: 8 (over z, x), seq: 4 (over y, core).
Axes of the slice: x: 2, y: 2, z: 4, core: 2. Of those that a mesh axis runs over, the one named last changes fastest.
Arguments:
- tokens: bfloat16 [16, 1376, 1024], P('shard', 'seq'), may hold values from -6 to 6
- valid_mask: int32 [16, 1376], P('shard'), may hold values from 0 to 1, as said below
- first_gain: bfloat16 [1024], P('shard'), may hold values from 0.5 to 1.5
- first_shift: bfloat16 [1024], P('shard'), may hold values from -1.5 to 1.5
- joint_weight: bfloat16 [1024, 3072], P('shard'), may hold values from -0.25 to 0.25
- query_bias: bfloat16 [1024], P('shard'), may hold values from -2.5 to 2.5
- value_bias: bfloat16 [1024], P('shard'), may hold values from -2.5 to 2.5
- output_weight: bfloat16 [1024, 1024], P('shard'), may hold values from -1.5 to 1.5
- output_bias: bfloat16 [1024], P('shard'), may hold values from -1.5 to 1.5
- scale_one: bfloat16 [1024], P('shard'), may hold values from 0.25 to 1.5
- second_gain: bfloat16 [1024], P('shard'), may hold values from 0.5 to 1.5
- second_shift: bfloat16 [1024], P('shard'), may hold values from -1.5 to 1.5
- expand_weight: bfloat16 [1024, 4096], P('shard'), may hold values from -0.1875 to 0.1875
- expand_bias: bfloat16 [4096], P('shard'), may hold values from -2.5 to 2.5
- reduce_weight: bfloat16 [4096, 1024], P('shard'), may hold values from -0.125 to 0.125
- reduce_bias: bfloat16 [1024], P('shard'), may hold values from -1.5 to 1.5
- scale_two: bfloat16 [1024], P('shard'), may hold values from 0.25 to 1.5
- cotangent: bfloat16 [16, 1376, 1024], P('shard', 'seq'), may hold values from -6 to 6
Outputs:
- layer_out: bfloat16 [16, 1376, 1024], P('shard', 'seq')
- tokens_grad: bfloat16 [16, 1376, 1024], P('shard', 'seq')
- grad_first_gain: float32 [1024], P('shard')
- grad_first_shift: float32 [1024], P('shard')
- grad_joint_weight: float32 [1024, 3072], P('shard')
- grad_query_bias: float32 [1024], P('shard')
- grad_value_bias: float32 [1024], P('shard')
- grad_output_weight: float32 [1024, 1024], P('shard')
- grad_output_bias: float32 [1024], P('shard')
- grad_scale_one: float32 [1024], P('shard')
- grad_second_gain: float32 [1024], P('shard')
- grad_second_shift: float32 [1024], P('shard')
- grad_expand_weight: float32 [1024, 4096], P('shard')
- grad_expand_bias: float32 [4096], P('shard')
- grad_reduce_weight: float32 [4096, 1024], P('shard')
- grad_reduce_bias: float32 [1024], P('shard')
- grad_scale_two: float32 [1024], P('shard')
The draws below stay inside these ranges and needn't reach their ends.
Inputs may be any that keep to these rules, and one draw needn't show every extreme that they name: `valid_mask`: in each image the slots with mask 1 form a prefix whose length lies between 1032 and 1370; both of these lengths occur in every draw; all other slots have mask 0.
All inputs are finite; a program needn't handle non-finite values.
Results may differ from the reference program's by a relative error of at most 0.015.
Values may be sent and summed in bfloat16 or wider, within the bound.
No kernel may reach another device: no remote copies, remote signals or barrier semaphores. Data moves between devices by JAX's collectives and lax.ppermute only.
A program may use at most 256 MiB of HBM per device.

```python
import math
import jax
import jax.numpy as jnp
from jax import lax

D = 1024
H = 16
HD = 64
FF = 4096
SEQ = 1376
IMAGES = 16


def draw_valid_mask(key, part):
    lengths = jax.random.randint(key, (IMAGES,), SEQ * 3 // 4, SEQ - 5)
    lengths = lengths.at[0].set(SEQ - 6).at[1].set(SEQ * 3 // 4)
    positions = jnp.arange(SEQ, dtype=jnp.int32)
    return (positions[None, :] < lengths[:, None]).astype(jnp.int32)


def block_scale(key, extent, cuts, least, top_value):
    def one(dim, blocks):
        draws = jax.random.uniform(jax.random.fold_in(jax.random.fold_in(key, 6), dim), (blocks,), jnp.float32, least / len(cuts), top_value / len(cuts))
        return jnp.repeat(jnp.exp(draws), extent[dim] // blocks).reshape((-1,) + (1,) * (len(extent) - dim - 1))

    loudness = one(*cuts[0])
    for cut in cuts[1:]:
        loudness = loudness * one(*cut)
    return loudness


def normal_values(rng, dims, width, most, cuts=(), kind=jnp.bfloat16):
    entries = width * jax.random.normal(rng, dims, jnp.float32)
    if cuts:
        entries = entries * block_scale(rng, dims, cuts, -0.22, 0.18)
    return jnp.clip(entries, -most, most).astype(kind)


def setup_inputs(seed: int = 0) -> dict:
    key_of = jax.random.split(jax.random.key(seed), 19)
    tokens = normal_values(key_of[0], (IMAGES, SEQ, D), 1.0, 6.0, ((0, 8), (1, 4)))
    valid_mask = draw_valid_mask(jax.random.fold_in(key_of[18], 71), 0)
    first_gain = jnp.clip(1.0 + 0.1 * jax.random.normal(key_of[2], (D,), jnp.float32), 0.5, 1.5).astype(jnp.bfloat16)
    first_shift = normal_values(key_of[3], (D,), 0.3, 1.5, ((0, 8),))
    joint_weight = normal_values(key_of[4], (D, 3 * D), (D // 2) ** -0.5, 0.25, ((0, 8),))
    query_bias = normal_values(key_of[5], (D,), 0.5, 2.5, ((0, 8),))
    value_bias = normal_values(key_of[6], (D,), 0.5, 2.5, ((0, 8),))
    output_weight = normal_values(key_of[7], (D, D), (max(D // 64, 1)) ** -0.5, 1.5, ((0, 8),))
    output_bias = normal_values(key_of[8], (D,), 0.3, 1.5, ((0, 8),))
    scale_one = jnp.clip(jnp.exp(math.log(1.5) - 1.7917595 * jax.random.uniform(key_of[9], (D,), jnp.float32) ** block_scale(key_of[9], (D,), ((0, 8),), -0.2, 0.2)), 0.25, 1.5).astype(jnp.bfloat16)
    second_gain = jnp.clip(1.0 + 0.1 * jax.random.normal(key_of[10], (D,), jnp.float32), 0.5, 1.5).astype(jnp.bfloat16)
    second_shift = normal_values(key_of[11], (D,), 0.3, 1.5, ((0, 8),))
    expand_weight = normal_values(key_of[12], (D, FF), D ** -0.5, 0.1875, ((0, 8),))
    expand_bias = normal_values(key_of[13], (FF,), 0.5, 2.5, ((0, 8),))
    reduce_weight = normal_values(key_of[14], (FF, D), (FF // 2) ** -0.5, 0.125, ((0, 8),))
    reduce_bias = normal_values(key_of[15], (D,), 0.3, 1.5, ((0, 8),))
    scale_two = jnp.clip(jnp.exp(math.log(1.5) - 1.7917595 * jax.random.uniform(key_of[16], (D,), jnp.float32) ** block_scale(key_of[16], (D,), ((0, 8),), -0.2, 0.2)), 0.25, 1.5).astype(jnp.bfloat16)
    cotangent = normal_values(key_of[17], (IMAGES, SEQ, D), 1.0, 6.0, ((0, 8), (1, 4)))
    return {"tokens": tokens, "valid_mask": valid_mask, "first_gain": first_gain, "first_shift": first_shift, "joint_weight": joint_weight, "query_bias": query_bias, "value_bias": value_bias, "output_weight": output_weight, "output_bias": output_bias, "scale_one": scale_one, "second_gain": second_gain, "second_shift": second_shift, "expand_weight": expand_weight, "expand_bias": expand_bias, "reduce_weight": reduce_weight, "reduce_bias": reduce_bias, "scale_two": scale_two, "cotangent": cotangent}


@jax.custom_vjp
def low(v):
    return lax.optimization_barrier(v.astype(jnp.bfloat16)).astype(jnp.float32)

@jax.custom_vjp
def low_back(v):
    return v

def low_keep(v):
    return (low(v), None)

def low_pass(kept, grad):
    return (grad,)

def back_keep(v):
    return (v, None)

def back_low(kept, grad):
    return (low(grad),)
low.defvjp(low_keep, low_pass)
low_back.defvjp(back_keep, back_low)
EPS = 1e-06
MASK_FILL = -1e+30
HIGHEST_PRECISION = lax.Precision.HIGHEST

def layer_norm(values, gain_vec, shift_vec):
    center = values - lax.optimization_barrier(jnp.mean(values, axis=-1, keepdims=True))
    spread = lax.optimization_barrier(jnp.mean(center * center, axis=-1, keepdims=True))
    return center * lax.rsqrt(spread + EPS) * gain_vec + shift_vec

def product(left, right):
    return jnp.dot(left, right, precision=HIGHEST_PRECISION)

def one_head(queries, key_rows, values, valid_keys):
    scores = low_back(product(queries, key_rows.T) * HD ** (-0.5))
    masked = jnp.where(valid_keys[None, :], scores, MASK_FILL)
    row_max = lax.optimization_barrier(jnp.max(masked, axis=-1, keepdims=True))
    exponent = jnp.exp(masked - row_max)
    probabilities = exponent / lax.optimization_barrier(jnp.sum(exponent, axis=-1, keepdims=True))
    return product(low(probabilities), values)

def split_heads(columns):
    return columns.reshape(SEQ, H, HD).transpose(1, 0, 2)

def layer_image(params, inputs, valid_keys):
    first_gain, first_shift, joint_weight, query_bias, value_bias, output_weight, output_bias, scale_one, second_gain, second_shift, expand_weight, expand_bias, reduce_weight, reduce_bias, scale_two = params
    normed = low(layer_norm(inputs, first_gain, first_shift))
    joint = product(normed, joint_weight)
    queries = low_back(low(joint[:, :D] + query_bias))
    key_rows = low_back(low(joint[:, D:2 * D]))
    values = low_back(low(joint[:, 2 * D:] + value_bias))

    def per_head(triple):
        return one_head(triple[0], triple[1], triple[2], valid_keys)
    heads_out = lax.map(jax.checkpoint(per_head), (split_heads(queries), split_heads(key_rows), split_heads(values)))
    attended = low_back(low(heads_out.transpose(1, 0, 2).reshape(SEQ, D)))
    mixed_out = low_back(product(attended, output_weight) + output_bias)
    middle = inputs + scale_one * mixed_out
    second_normed = low(layer_norm(middle, second_gain, second_shift))
    hidden = low_back(product(second_normed, expand_weight) + expand_bias)
    active = low(jax.nn.gelu(hidden, approximate=False))
    branch = low_back(product(active, reduce_weight) + reduce_bias)
    return middle + scale_two * branch

def reference(tokens, valid_mask, first_gain, first_shift, joint_weight, query_bias, value_bias, output_weight, output_bias, scale_one, second_gain, second_shift, expand_weight, expand_bias, reduce_weight, reduce_bias, scale_two, cotangent):
    params = tuple((element.astype(jnp.float32) for element in (first_gain, first_shift, joint_weight, query_bias, value_bias, output_weight, output_bias, scale_one, second_gain, second_shift, expand_weight, expand_bias, reduce_weight, reduce_bias, scale_two)))
    zero_grads = tuple((jnp.zeros_like(element) for element in params))

    def step(running, element):
        image_tokens, mask_row, image_back = element
        valid_keys = mask_row > 0

        def apply_layer(weights, inputs):
            return layer_image(weights, inputs, valid_keys)
        result, pullback = jax.vjp(apply_layer, params, image_tokens.astype(jnp.float32))
        weight_grads, input_grad = pullback(image_back.astype(jnp.float32))
        running = jax.tree.map(lambda left, right: left + right, running, weight_grads)
        return (running, (result.astype(jnp.bfloat16), input_grad.astype(jnp.bfloat16)))
    totals, outputs = lax.scan(step, zero_grads, (tokens, valid_mask, cotangent))
    return (outputs[0], outputs[1], totals[0], totals[1], totals[2], totals[3], totals[4], totals[5], totals[6], totals[7], totals[8], totals[9], totals[10], totals[11], totals[12], totals[13], totals[14])
```

```python
import functools

import jax
import jax.numpy as jnp
from jax import lax
from jax.experimental import pallas as pl
from jax.experimental.pallas import tpu as pltpu
from jax.sharding import PartitionSpec as P

HD = 64
EPS = 1e-06
MASK_FILL = -1e30
F32 = jnp.float32
BF16 = jnp.bfloat16
BOTH = ("shard", "seq")
VMEM_LIMIT = 60 * 1024 * 1024


def chunks_of(total, size):
    return [(start, min(size, total - start)) for start in range(0, total, size)]


def lane_half(shape, half):
    lanes = lax.broadcasted_iota(jnp.int32, shape, 1)
    return (lanes < HD) if half == 0 else (lanes >= HD)


def attention_forward_kernel(qkv_ref, bias_ref, out_ref, lse_ref):
    rows = qkv_ref.shape[0]
    keys = qkv_ref[:, 128:256]
    bias = bias_ref[...]
    zero = jnp.zeros((), BF16)
    values = [
        jnp.where(lane_half((rows, 128), half), qkv_ref[:, 256:384], zero) for half in range(2)
    ]
    for start, size in chunks_of(rows, 256):
        queries = qkv_ref[start : start + size, 0:128] * jnp.asarray(HD**-0.5, BF16)
        total = jnp.zeros((size, 128), F32)
        for half in range(2):
            own = jnp.where(lane_half((size, 128), half), queries, zero)
            scores = lax.dot_general(
                own, keys, (((1,), (1,)), ((), ())), preferred_element_type=F32
            )
            scores = scores + bias
            top = jnp.max(scores, axis=-1, keepdims=True)
            exponent = jnp.exp(scores - top)
            row_sum = jnp.sum(exponent, axis=-1, keepdims=True)
            part = jnp.dot(exponent.astype(BF16), values[half], preferred_element_type=F32)
            total = total + part * (1.0 / row_sum)
            log_total = top + jnp.log(row_sum)
            turned = jnp.transpose(jnp.broadcast_to(log_total, (size, 128)))
            lse_ref[0, half : half + 1, start : start + size] = turned[0:1, :]
        out_ref[start : start + size, :] = total.astype(BF16)


def attention_forward(qkv, bias_row):
    rows, columns = qkv.shape
    pairs = columns // 384
    return pl.pallas_call(
        attention_forward_kernel,
        out_shape=(
            jax.ShapeDtypeStruct((rows, pairs * 128), BF16),
            jax.ShapeDtypeStruct((pairs, 8, rows), F32),
        ),
        grid=(pairs,),
        in_specs=[
            pl.BlockSpec((rows, 384), lambda p: (0, p)),
            pl.BlockSpec((1, rows), lambda p: (0, 0)),
        ],
        out_specs=(
            pl.BlockSpec((rows, 128), lambda p: (0, p)),
            pl.BlockSpec((1, 8, rows), lambda p: (p, 0, 0)),
        ),
        compiler_params=pltpu.CompilerParams(vmem_limit_bytes=VMEM_LIMIT),
        name="attend",
    )(qkv, bias_row)


def attention_backward_kernel(
    qkv_ref, grad_ref, lse_ref, bias_ref, out_ref, key_acc, value_acc
):
    rows = qkv_ref.shape[0]
    scale = jnp.asarray(HD**-0.5, BF16)
    zero = jnp.zeros((), BF16)
    keys = qkv_ref[:, 128:256]
    values = qkv_ref[:, 256:384]
    masked_keys = [jnp.where(lane_half((rows, 128), half), keys * scale, zero) for half in range(2)]
    bias = bias_ref[...]
    contract_lanes = (((1,), (1,)), ((), ()))
    for index, (start, size) in enumerate(chunks_of(rows, 256)):
        queries = qkv_ref[start : start + size, 0:128] * scale
        grads = grad_ref[start : start + size, :]
        grad_queries = jnp.zeros((size, 128), F32)
        key_part = jnp.zeros((rows, 128), F32)
        value_part = jnp.zeros((rows, 128), F32)
        for half in range(2):
            mask = lane_half((size, 128), half)
            own = jnp.where(mask, queries, zero)
            own_grads = jnp.where(mask, grads, zero)
            scores = lax.dot_general(keys, own, contract_lanes, preferred_element_type=F32)
            probs = jnp.exp(scores + bias - lse_ref[0, half : half + 1, start : start + size])
            grad_probs = lax.dot_general(
                values, own_grads, contract_lanes, preferred_element_type=F32
            )
            inner = jnp.sum(probs * grad_probs, axis=0, keepdims=True)
            grad_scores = (probs * (grad_probs - inner)).astype(BF16)
            value_part += jnp.dot(probs.astype(BF16), own_grads, preferred_element_type=F32)
            key_part += jnp.dot(grad_scores, own, preferred_element_type=F32)
            grad_queries += lax.dot_general(
                grad_scores, masked_keys[half], (((0,), (0,)), ((), ())), preferred_element_type=F32
            )
        if index == 0:
            key_acc[...] = key_part
            value_acc[...] = value_part
        else:
            key_acc[...] += key_part
            value_acc[...] += value_part
        out_ref[start : start + size, 0:128] = grad_queries.astype(BF16)
    out_ref[:, 128:256] = key_acc[...].astype(BF16)
    out_ref[:, 256:384] = value_acc[...].astype(BF16)


def attention_backward(qkv, grads, log_total, bias_column):
    rows, columns = qkv.shape
    pairs = columns // 384
    return pl.pallas_call(
        attention_backward_kernel,
        out_shape=jax.ShapeDtypeStruct((rows, columns), BF16),
        grid=(pairs,),
        in_specs=[
            pl.BlockSpec((rows, 384), lambda p: (0, p)),
            pl.BlockSpec((rows, 128), lambda p: (0, p)),
            pl.BlockSpec((1, 8, rows), lambda p: (p, 0, 0)),
            pl.BlockSpec((rows, 1), lambda p: (0, 0)),
        ],
        out_specs=pl.BlockSpec((rows, 384), lambda p: (0, p)),
        scratch_shapes=[pltpu.VMEM((rows, 128), F32), pltpu.VMEM((rows, 128), F32)],
        compiler_params=pltpu.CompilerParams(vmem_limit_bytes=VMEM_LIMIT),
        name="attend_back",
    )(qkv, grads, log_total, bias_column)


class Place:
    def __init__(self, shards):
        self.shards = shards
        self.bits = shards.bit_length() - 1
        self.shard = lax.axis_index("shard")
        seq = lax.axis_index("seq")
        self.y = seq // 2
        self.c = seq % 2
        self.x = self.shard % 2

    def bit(self, index):
        return (self.shard // (1 << index)) % 2

    def swap(self, value, shard_flip=0, seq_flip=0):
        pairs = [
            (s * 4 + q, (s ^ shard_flip) * 4 + (q ^ seq_flip))
            for s in range(self.shards)
            for q in range(4)
        ]
        return lax.ppermute(value, BOTH, pairs)

    def core(self, value):
        return self.swap(value, 0, 1)

    def over_y(self, value):
        return self.swap(value, 0, 2)

    def over_x(self, value):
        return self.swap(value, 1, 0)


def ordered(first, own, other, axis=0):
    return jnp.where(
        first == 0,
        jnp.concatenate([own, other], axis=axis),
        jnp.concatenate([other, own], axis=axis),
    )


def pick(value, index, axis):
    return lax.dynamic_index_in_dim(value, index, axis, keepdims=False)


def spread(place, piece):
    held = piece[None]
    for bit in range(1, place.bits):
        held = ordered(place.bit(bit), held, place.swap(held, 1 << bit))
    half = piece.shape[1] // 2
    first, second = held[:, :, :half], held[:, :, half:]
    first_x = place.over_x(first)
    second_y = place.over_y(second)
    return (
        (first, 0, 0, 0),
        (first_x, 1, 0, 0),
        (place.over_y(first), 0, 1, 0),
        (place.over_y(first_x), 1, 1, 0),
        (second, 0, 0, 1),
        (second_y, 0, 1, 1),
        (place.over_x(second), 1, 0, 1),
        (place.over_x(second_y), 1, 1, 1),
    )


def assemble_kernel(flips, plans, *refs):
    count = len(flips)
    place_ref, sources = refs[0], refs[1 : 1 + count]
    outputs = refs[1 + count : 1 + count + len(plans)]
    sem = refs[-1]
    x, y = place_ref[0], place_ref[1]
    copies = []
    for source, (flip_x, flip_y, half) in zip(sources, flips):
        to_x = lax.rem(x + flip_x, 2)
        to_y = lax.rem(y + flip_y, 2)
        for output, (kind, column, width) in zip(outputs, plans):
            if kind == "columns":
                at = pl.multiple_of(to_y * (2 * width) + half * width, 128)
                target = output.at[:, to_x, :, pl.ds(at, width)]
            else:
                target = output.at[:, to_x, to_y, :, pl.ds(half * width, width)]
            copies.append(
                pltpu.make_async_copy(
                    source.at[:, :, pl.ds(column, width)], target, sem.at[len(copies)]
                )
            )
    for copy in copies:
        copy.start()
    for copy in copies:
        copy.wait()


def assemble(place, pieces, plans, name):
    arrays = [piece[0] for piece in pieces]
    flips = [piece[1:] for piece in pieces]
    outer, rows, _ = arrays[0].shape
    shapes = []
    for kind, _, width in plans:
        if kind == "columns":
            shapes.append(jax.ShapeDtypeStruct((outer, 2, rows, 4 * width), BF16))
        else:
            shapes.append(jax.ShapeDtypeStruct((outer, 2, 2, rows, 2 * width), BF16))
    where = jnp.stack([place.x, place.y]).astype(jnp.int32)
    outputs = pl.pallas_call(
        functools.partial(assemble_kernel, flips, plans),
        out_shape=shapes,
        grid_spec=pltpu.PrefetchScalarGridSpec(
            num_scalar_prefetch=1,
            grid=(1,),
            in_specs=[pl.BlockSpec(memory_space=pl.ANY)] * len(arrays),
            out_specs=[pl.BlockSpec(memory_space=pl.ANY)] * len(plans),
            scratch_shapes=[pltpu.SemaphoreType.DMA((len(arrays) * len(plans),))],
        ),
        name=name,
    )(where, *arrays)
    return [out.reshape(-1, out.shape[-1]) for out in outputs]


def step_down(place, value, axis, index, move):
    sent = pick(value, 1 - index, axis).astype(BF16)
    return pick(value, index, axis).astype(F32) + move(sent).astype(F32)


def collect(place, first, second):
    first = step_down(place, step_down(place, first, 1, place.x, place.over_x), 1, place.y, place.over_y)
    second = step_down(place, step_down(place, second, 2, place.y, place.over_y), 1, place.x, place.over_x)
    held = jnp.concatenate([first, second], axis=-1)
    for bit in range(place.bits - 1, 0, -1):
        held = held.reshape((2, -1) + held.shape[1:])
        held = step_down(
            place, held, 0, place.bit(bit), lambda v, b=bit: place.swap(v, 1 << b)
        )
    return held.reshape(held.shape[-2:])


def share(place, piece):
    piece = piece.astype(BF16)
    both = ordered(place.y, piece[None], place.over_y(piece)[None])
    return ordered(place.c, both[None], place.core(both)[None])


def normalize(values):
    center = values - jnp.mean(values, axis=-1, keepdims=True)
    inverse = lax.rsqrt(jnp.mean(center * center, axis=-1, keepdims=True) + EPS)
    return center * inverse, inverse


def norm_pull(grad, unit, inverse, gain):
    scaled = grad * gain
    return inverse * (
        scaled
        - jnp.mean(scaled, axis=-1, keepdims=True)
        - unit * jnp.mean(scaled * unit, axis=-1, keepdims=True)
    )


def dot(left, right, dims=((1,), (0,))):
    return lax.dot_general(left, right, (dims, ((), ())), preferred_element_type=F32)


NAMES = (
    "first_gain",
    "first_shift",
    "query_bias",
    "value_bias",
    "output_bias",
    "scale_one",
    "second_gain",
    "second_shift",
    "reduce_bias",
    "scale_two",
    "expand_bias",
)


def body(
    tokens,
    valid_mask,
    first_gain,
    first_shift,
    joint_weight,
    query_bias,
    value_bias,
    output_weight,
    output_bias,
    scale_one,
    second_gain,
    second_shift,
    expand_weight,
    expand_bias,
    reduce_weight,
    reduce_bias,
    scale_two,
    cotangent,
):
    shards = lax.axis_size("shard")
    place = Place(shards)
    c, y = place.c, place.y
    slab, width = joint_weight.shape[0], tokens.shape[2]
    local = tokens.shape[1]
    mine_rows = 2 * local
    hidden_width = expand_weight.shape[1]
    part = slab

    own_vectors = {
        "first_gain": first_gain,
        "first_shift": first_shift,
        "query_bias": query_bias,
        "value_bias": value_bias,
        "output_bias": output_bias,
        "scale_one": scale_one,
        "second_gain": second_gain,
        "second_shift": second_shift,
        "reduce_bias": reduce_bias,
        "scale_two": scale_two,
        "expand_bias": expand_bias,
    }
    packed = jnp.concatenate([own_vectors[name] for name in NAMES])[None]
    for bit in range(place.bits):
        packed = ordered(place.bit(bit), packed, place.swap(packed, 1 << bit))
    vectors = {}
    offset = 0
    for name in NAMES:
        size = own_vectors[name].shape[0]
        block = packed[:, offset : offset + size].astype(F32)
        offset += size
        if name == "expand_bias":
            block = pick(block.reshape(shards, 2, size // 2), c, 1)
        vectors[name] = block.reshape(-1)

    joint_piece = joint_weight.reshape(slab, 3, 2, 2, 2, 128).transpose(2, 3, 0, 4, 1, 5)
    joint_piece = pick(pick(joint_piece, c, 0), y, 0).reshape(slab, 768)
    out_piece = pick(pick(output_weight.reshape(slab, 2, 2, 2, 128), c, 1), y, 1)
    expand_own = pick(
        expand_weight.reshape(slab, shards, 2, hidden_width // (2 * shards)), c, 2
    ).reshape(slab, 2, 2, hidden_width // 8)
    expand_piece = pick(expand_own, y, 1)
    mixed_piece = jnp.concatenate([out_piece, expand_piece], axis=-1).reshape(slab, -1)
    reduce_piece = pick(pick(reduce_weight.reshape(2, 2, slab, width), c, 0), y, 0)

    def to_image(array):
        own, other = pick(array, y, 0), pick(array, 1 - y, 0)
        return jnp.concatenate([own, place.over_y(other)], axis=0)

    def from_image(array):
        own, other = array[:local], place.over_y(array[local:])
        return ordered(y, own[None], other[None])

    mine = to_image(tokens)
    joint_pieces = spread(place, joint_piece)
    both = jnp.concatenate([mine, place.core(mine)], axis=0)
    (joint_own,) = assemble(place, joint_pieces, [("columns", 0, 384)], "lay_joint")
    mixed_pieces = spread(place, mixed_piece)
    out_own, expand_full = assemble(
        place, mixed_pieces, [("columns", 0, 128), ("columns", 128, 512)], "lay_mixed"
    )
    reduce_pieces = spread(place, reduce_piece)
    (reduce_full,) = assemble(place, reduce_pieces, [("rows", 0, 512)], "lay_reduce")
    out_full = ordered(c, out_own, place.core(out_own), axis=1)
    back_mine = to_image(cotangent)
    back_both = jnp.concatenate([back_mine, place.core(back_mine)], axis=0)

    mask = pick(valid_mask, y, 0).reshape(4, local)
    mask = jnp.concatenate(
        [pick(mask, index, 0) for index in (2 * y + c, 2 - 2 * y + c, 2 * y + 1 - c, 3 - 2 * y - c)]
    )
    bias = jnp.where(mask > 0, 0.0, MASK_FILL).astype(F32)

    gain_one, shift_one = vectors["first_gain"], vectors["first_shift"]
    unit_both, _ = normalize(both.astype(F32))
    normed = (unit_both * gain_one + shift_one).astype(BF16)
    heads_of = lambda vector: pick(vector.reshape(2, 4, 128), c, 0)
    query_part, value_part = heads_of(vectors["query_bias"]), heads_of(vectors["value_bias"])
    joint_bias = jnp.stack([query_part, jnp.zeros_like(query_part), value_part], axis=1).reshape(-1)
    projected = (dot(normed, joint_own) + joint_bias).astype(BF16)
    attended, log_total = attention_forward(projected, bias[None, :])
    merged = ordered(c, attended[:mine_rows], place.core(attended[mine_rows:]), axis=1)
    mixed_out = dot(merged, out_full) + vectors["output_bias"]
    middle = mine.astype(F32) + vectors["scale_one"] * mixed_out
    unit_two, inverse_two = normalize(middle)
    second_normed = (unit_two * vectors["second_gain"] + vectors["second_shift"]).astype(BF16)

    second_both = jnp.concatenate([second_normed, place.core(second_normed)], axis=0)
    hidden = dot(second_both, expand_full) + vectors["expand_bias"]
    cumulative = 0.5 * (1.0 + lax.erf(hidden * 2**-0.5))
    active = (hidden * cumulative).astype(BF16)
    slope = (cumulative + hidden * (jnp.exp(-0.5 * hidden * hidden) * 0.3989422804014327)).astype(
        BF16
    )
    branch_parts = dot(active, reduce_full)
    branch = (
        branch_parts[:mine_rows]
        + place.core(branch_parts[mine_rows:].astype(BF16)).astype(F32)
        + vectors["reduce_bias"]
    )
    layer_out = from_image((middle + vectors["scale_two"] * branch).astype(BF16))

    grads = {}
    grad_out = back_mine.astype(F32)
    grads["scale_two"] = jnp.sum(grad_out * branch, axis=0)
    grad_branch = (back_both.astype(F32) * vectors["scale_two"]).astype(BF16)
    grads["reduce_bias"] = jnp.sum(grad_branch[:mine_rows].astype(F32), axis=0)
    grad_active = dot(grad_branch, reduce_full, ((1,), (1,)))
    grad_hidden = (grad_active * slope.astype(F32)).astype(BF16)
    grad_reduce = dot(active, grad_branch, ((0,), (0,)))
    expand_bias_grad = jnp.sum(grad_hidden.astype(F32), axis=0)
    grad_expand = dot(second_both, grad_hidden, ((0,), (0,)))
    second_parts = dot(grad_hidden, expand_full, ((1,), (1,)))
    grad_second = second_parts[:mine_rows] + place.core(
        second_parts[mine_rows:].astype(BF16)
    ).astype(F32)
    grads["second_gain"] = jnp.sum(grad_second * unit_two, axis=0)
    grads["second_shift"] = jnp.sum(grad_second, axis=0)
    grad_middle = grad_out + norm_pull(grad_second, unit_two, inverse_two, vectors["second_gain"])
    grads["scale_one"] = jnp.sum(grad_middle * mixed_out, axis=0)
    grad_mixed = (grad_middle * vectors["scale_one"]).astype(BF16)
    grads["output_bias"] = jnp.sum(grad_mixed.astype(F32), axis=0)
    grad_merged = dot(grad_mixed, out_full, ((1,), (1,))).astype(BF16).reshape(mine_rows, 2, -1)
    grad_heads = jnp.concatenate(
        [pick(grad_merged, c, 1), place.core(pick(grad_merged, 1 - c, 1))], axis=0
    )
    grad_output = dot(merged, grad_mixed, ((0,), (0,))).reshape(width, 2, width // 2)
    grad_output = step_down(place, grad_output, 1, c, place.core)
    grad_projected = attention_backward(projected, grad_heads, log_total, bias[:, None])
    column_sums = jnp.sum(grad_projected.astype(F32), axis=0).reshape(4, 3, 128)
    grad_joint = dot(normed, grad_projected, ((0,), (0,)))
    first_parts = dot(grad_projected, joint_own, ((1,), (1,)))
    grad_first = first_parts[:mine_rows] + place.core(first_parts[mine_rows:].astype(BF16)).astype(
        F32
    )
    unit_one, inverse_one = normalize(mine.astype(F32))
    grads["first_gain"] = jnp.sum(grad_first * unit_one, axis=0)
    grads["first_shift"] = jnp.sum(grad_first, axis=0)
    tokens_grad = from_image(
        (grad_middle + norm_pull(grad_first, unit_one, inverse_one, gain_one)).astype(BF16)
    )

    outer = shards // 2
    quarter = hidden_width // 8
    reduce_view = grad_reduce.reshape(outer, 2, 2, slab, 2, width // 2)
    reduce_sum = collect(place, reduce_view[..., 0, :], reduce_view[..., 1, :])
    expand_view = grad_expand.reshape(outer, 2, slab, 2, 2, quarter).transpose(0, 1, 3, 2, 4, 5)
    out_view = grad_output.reshape(outer, 2, slab, 2, 2, 128).transpose(0, 1, 3, 2, 4, 5)
    mixed_sum = collect(
        place,
        jnp.concatenate([out_view[..., 0, :], expand_view[..., 0, :]], axis=-1),
        jnp.concatenate([out_view[..., 1, :], expand_view[..., 1, :]], axis=-1),
    )
    joint_view = grad_joint.reshape(outer, 2, slab, 2, 2, 384).transpose(0, 1, 3, 2, 4, 5)
    joint_sum = collect(place, joint_view[..., 0, :], joint_view[..., 1, :])

    reduce_grad = share(place, reduce_sum).reshape(4 * slab, width).astype(F32)
    mixed_all = share(place, mixed_sum).reshape(2, 2, slab, 2, 128 + quarter)
    out_grad = mixed_all[..., :128].transpose(2, 0, 1, 3, 4).reshape(slab, width).astype(F32)
    expand_grad = mixed_all[..., 128:].transpose(0, 2, 1, 3, 4).reshape(2, slab, shards, -1)
    expand_grad = expand_grad.transpose(1, 2, 0, 3).reshape(slab, hidden_width).astype(F32)
    joint_grad = share(place, joint_sum).reshape(2, 2, slab, 2, 3, 128)
    joint_grad = joint_grad.transpose(2, 4, 0, 1, 3, 5).reshape(slab, 3 * width).astype(F32)

    def half_of(block, groups):
        zeros = jnp.zeros_like(block)
        return ordered(c, block[:, None], zeros[:, None], axis=1).reshape(groups, -1)

    grads["query_bias"] = half_of(column_sums[:, 0, :].reshape(1, -1), 1).reshape(-1)
    grads["value_bias"] = half_of(column_sums[:, 2, :].reshape(1, -1), 1).reshape(-1)
    grads["expand_bias"] = half_of(expand_bias_grad.reshape(shards, -1), shards).reshape(-1)
    totals = jnp.concatenate([grads[name].reshape(shards, -1) for name in NAMES], axis=1)
    for bit in range(place.bits - 1, -1, -1):
        totals = totals.reshape((2, -1) + totals.shape[1:])
        totals = pick(totals, place.bit(bit), 0) + place.swap(
            pick(totals, 1 - place.bit(bit), 0), 1 << bit
        )
    totals = totals.reshape(-1)
    totals = totals + place.over_y(totals)
    totals = totals + place.core(totals)
    shares = {}
    offset = 0
    for name in NAMES:
        size = own_vectors[name].shape[0]
        shares[name] = totals[offset : offset + size]
        offset += size

    return (
        layer_out,
        tokens_grad,
        shares["first_gain"],
        shares["first_shift"],
        joint_grad,
        shares["query_bias"],
        shares["value_bias"],
        out_grad,
        shares["output_bias"],
        shares["scale_one"],
        shares["second_gain"],
        shares["second_shift"],
        expand_grad,
        shares["expand_bias"],
        reduce_grad,
        shares["reduce_bias"],
        shares["scale_two"],
    )


def solution(mesh):
    row, rows = P("shard"), P("shard", None)
    image = P("shard", "seq", None)
    return jax.shard_map(
        body,
        mesh=mesh,
        in_specs=(
            image, rows, row, row, rows, row, row, rows, row, row, row, row, rows, row, rows, row, row, image,
        ),
        out_specs=(
            image, image, row, row, rows, row, row, rows, row, row, row, row, rows, row, rows, row, row,
        ),
        check_vma=False,
    )
```

```python
import functools

import jax
import jax.numpy as jnp
from jax import lax
from jax.experimental import pallas as pl
from jax.experimental.pallas import tpu as pltpu
from jax.sharding import PartitionSpec as P

HD = 64
EPS = 1e-06
MASK_FILL = -1e30
F32 = jnp.float32
BF16 = jnp.bfloat16
BOTH = ("shard", "seq")
VMEM_LIMIT = 60 * 1024 * 1024


def chunks_of(total, size):
    return [(start, min(size, total - start)) for start in range(0, total, size)]


def lane_half(shape, half):
    lanes = lax.broadcasted_iota(jnp.int32, shape, 1)
    return (lanes < HD) if half == 0 else (lanes >= HD)


def attention_forward_kernel(qkv_ref, bias_ref, out_ref, lse_ref):
    rows = qkv_ref.shape[0]
    keys = qkv_ref[:, 128:256]
    bias = bias_ref[...]
    zero = jnp.zeros((), BF16)
    values = [
        jnp.where(lane_half((rows, 128), half), qkv_ref[:, 256:384], zero) for half in range(2)
    ]
    for start, size in chunks_of(rows, 256):
        queries = qkv_ref[start : start + size, 0:128] * jnp.asarray(HD**-0.5, BF16)
        total = jnp.zeros((size, 128), F32)
        for half in range(2):
            own = jnp.where(lane_half((size, 128), half), queries, zero)
            scores = lax.dot_general(
                own, keys, (((1,), (1,)), ((), ())), preferred_element_type=F32
            )
            scores = scores + bias
            top = jnp.max(scores, axis=-1, keepdims=True)
            exponent = jnp.exp(scores - top)
            row_sum = jnp.sum(exponent, axis=-1, keepdims=True)
            part = jnp.dot(exponent.astype(BF16), values[half], preferred_element_type=F32)
            total = total + part * (1.0 / row_sum)
            log_total = top + jnp.log(row_sum)
            turned = jnp.transpose(jnp.broadcast_to(log_total, (size, 128)))
            lse_ref[0, half : half + 1, start : start + size] = turned[0:1, :]
        out_ref[start : start + size, :] = total.astype(BF16)


def attention_forward(qkv, bias_row):
    rows, columns = qkv.shape
    pairs = columns // 384
    return pl.pallas_call(
        attention_forward_kernel,
        out_shape=(
            jax.ShapeDtypeStruct((rows, pairs * 128), BF16),
            jax.ShapeDtypeStruct((pairs, 8, rows), F32),
        ),
        grid=(pairs,),
        in_specs=[
            pl.BlockSpec((rows, 384), lambda p: (0, p)),
            pl.BlockSpec((1, rows), lambda p: (0, 0)),
        ],
        out_specs=(
            pl.BlockSpec((rows, 128), lambda p: (0, p)),
            pl.BlockSpec((1, 8, rows), lambda p: (p, 0, 0)),
        ),
        compiler_params=pltpu.CompilerParams(vmem_limit_bytes=VMEM_LIMIT),
        name="attend",
    )(qkv, bias_row)


def attention_backward_kernel(
    qkv_ref, grad_ref, lse_ref, bias_ref, out_ref, key_acc, value_acc
):
    rows = qkv_ref.shape[0]
    scale = jnp.asarray(HD**-0.5, BF16)
    zero = jnp.zeros((), BF16)
    keys = qkv_ref[:, 128:256]
    values = qkv_ref[:, 256:384]
    masked_keys = [jnp.where(lane_half((rows, 128), half), keys * scale, zero) for half in range(2)]
    bias = bias_ref[...]
    contract_lanes = (((1,), (1,)), ((), ()))
    for index, (start, size) in enumerate(chunks_of(rows, 256)):
        queries = qkv_ref[start : start + size, 0:128] * scale
        grads = grad_ref[start : start + size, :]
        grad_queries = jnp.zeros((size, 128), F32)
        key_part = jnp.zeros((rows, 128), F32)
        value_part = jnp.zeros((rows, 128), F32)
        for half in range(2):
            mask = lane_half((size, 128), half)
            own = jnp.where(mask, queries, zero)
            own_grads = jnp.where(mask, grads, zero)
            scores = lax.dot_general(keys, own, contract_lanes, preferred_element_type=F32)
            probs = jnp.exp(scores + bias - lse_ref[0, half : half + 1, start : start + size])
            grad_probs = lax.dot_general(
                values, own_grads, contract_lanes, preferred_element_type=F32
            )
            inner = jnp.sum(probs * grad_probs, axis=0, keepdims=True)
            grad_scores = (probs * (grad_probs - inner)).astype(BF16)
            value_part += jnp.dot(probs.astype(BF16), own_grads, preferred_element_type=F32)
            key_part += jnp.dot(grad_scores, own, preferred_element_type=F32)
            grad_queries += lax.dot_general(
                grad_scores, masked_keys[half], (((0,), (0,)), ((), ())), preferred_element_type=F32
            )
        if index == 0:
            key_acc[...] = key_part
            value_acc[...] = value_part
        else:
            key_acc[...] += key_part
            value_acc[...] += value_part
        out_ref[start : start + size, 0:128] = grad_queries.astype(BF16)
    out_ref[:, 128:256] = key_acc[...].astype(BF16)
    out_ref[:, 256:384] = value_acc[...].astype(BF16)


def attention_backward(qkv, grads, log_total, bias_column):
    rows, columns = qkv.shape
    pairs = columns // 384
    return pl.pallas_call(
        attention_backward_kernel,
        out_shape=jax.ShapeDtypeStruct((rows, columns), BF16),
        grid=(pairs,),
        in_specs=[
            pl.BlockSpec((rows, 384), lambda p: (0, p)),
            pl.BlockSpec((rows, 128), lambda p: (0, p)),
            pl.BlockSpec((1, 8, rows), lambda p: (p, 0, 0)),
            pl.BlockSpec((rows, 1), lambda p: (0, 0)),
        ],
        out_specs=pl.BlockSpec((rows, 384), lambda p: (0, p)),
        scratch_shapes=[pltpu.VMEM((rows, 128), F32), pltpu.VMEM((rows, 128), F32)],
        compiler_params=pltpu.CompilerParams(vmem_limit_bytes=VMEM_LIMIT),
        name="attend_back",
    )(qkv, grads, log_total, bias_column)


class Place:
    def __init__(self, shards):
        self.shards = shards
        self.bits = shards.bit_length() - 1
        self.shard = lax.axis_index("shard")
        seq = lax.axis_index("seq")
        self.y = seq // 2
        self.c = seq % 2
        self.x = self.shard % 2

    def bit(self, index):
        return (self.shard // (1 << index)) % 2

    def swap(self, value, shard_flip=0, seq_flip=0):
        pairs = [
            (s * 4 + q, (s ^ shard_flip) * 4 + (q ^ seq_flip))
            for s in range(self.shards)
            for q in range(4)
        ]
        return lax.ppermute(value, BOTH, pairs)

    def core(self, value):
        return self.swap(value, 0, 1)

    def over_y(self, value):
        return self.swap(value, 0, 2)

    def over_x(self, value):
        return self.swap(value, 1, 0)


def ordered(first, own, other, axis=0):
    return jnp.where(
        first == 0,
        jnp.concatenate([own, other], axis=axis),
        jnp.concatenate([other, own], axis=axis),
    )


def pick(value, index, axis):
    return lax.dynamic_index_in_dim(value, index, axis, keepdims=False)


def spread(place, piece):
    held = piece[None]
    for bit in range(1, place.bits):
        held = ordered(place.bit(bit), held, place.swap(held, 1 << bit))
    half = piece.shape[1] // 2
    first, second = held[:, :, :half], held[:, :, half:]
    first_x = place.over_x(first)
    second_y = place.over_y(second)
    return (
        (first, 0, 0, 0),
        (first_x, 1, 0, 0),
        (place.over_y(first), 0, 1, 0),
        (place.over_y(first_x), 1, 1, 0),
        (second, 0, 0, 1),
        (second_y, 0, 1, 1),
        (place.over_x(second), 1, 0, 1),
        (place.over_x(second_y), 1, 1, 1),
    )


def assemble_kernel(flips, plans, place_ref, *refs):
    count = len(flips)
    sources, outputs = refs[:count], refs[count:]
    x, y = place_ref[0], place_ref[1]
    for source, (flip_x, flip_y, half) in zip(sources, flips):
        to_x = lax.rem(x + flip_x, 2)
        to_y = lax.rem(y + flip_y, 2)
        for output, (kind, column, width) in zip(outputs, plans):
            value = source[0, :, column : column + width]
            if kind == "columns":
                at = pl.multiple_of(to_y * (2 * width) + half * width, 128)
                output[0, to_x, :, pl.ds(at, width)] = value
            else:
                output[0, to_x, to_y, :, half * width : (half + 1) * width] = value


def assemble(place, pieces, plans, name):
    arrays = [piece[0] for piece in pieces]
    flips = [piece[1:] for piece in pieces]
    outer, rows, columns = arrays[0].shape
    blocks = []
    for kind, _, width in plans:
        blocks.append((2, rows, 4 * width) if kind == "columns" else (2, 2, rows, 2 * width))

    def whole(block):
        zeros = (0,) * len(block)
        return pl.BlockSpec((1,) + block, lambda i, where: (i,) + zeros)

    where = jnp.stack([place.x, place.y]).astype(jnp.int32)
    outputs = pl.pallas_call(
        functools.partial(assemble_kernel, flips, plans),
        out_shape=[jax.ShapeDtypeStruct((outer,) + block, BF16) for block in blocks],
        grid_spec=pltpu.PrefetchScalarGridSpec(
            num_scalar_prefetch=1,
            grid=(outer,),
            in_specs=[whole((rows, columns))] * len(arrays),
            out_specs=[whole(block) for block in blocks],
        ),
        name=name,
    )(where, *arrays)
    return [out.reshape(-1, out.shape[-1]) for out in outputs]


def step_down(place, value, axis, index, move):
    sent = pick(value, 1 - index, axis).astype(BF16)
    return pick(value, index, axis).astype(F32) + move(sent).astype(F32)


def choose(index, values):
    return jnp.where(index == 0, *values), jnp.where(index == 0, *values[::-1])


def collect(place, first, second):
    def over(index, move, kept_sent):
        kept, sent = kept_sent
        return kept.astype(F32) + move(sent.astype(BF16)).astype(F32)

    def halve_x(value):
        return pick(value, place.x, 1), pick(value, 1 - place.x, 1)

    parts = [halve_x(value) for value in first]
    moved = place.over_x(jnp.stack([part[1].astype(BF16) for part in parts]))
    first = [part[0] + moved[i].astype(F32) for i, part in enumerate(parts)]
    first = over(place.y, place.over_y, choose(place.y, first))
    second = over(place.y, place.over_y, choose(place.y, second))
    second = over(place.x, place.over_x, halve_x(second))
    held = jnp.concatenate([first, second], axis=-1)
    for bit in range(place.bits - 1, 0, -1):
        held = held.reshape((2, -1) + held.shape[1:])
        held = step_down(
            place, held, 0, place.bit(bit), lambda v, b=bit: place.swap(v, 1 << b)
        )
    return held.reshape(held.shape[-2:])


def share(place, piece):
    piece = piece.astype(BF16)
    both = ordered(place.y, piece[None], place.over_y(piece)[None])
    return ordered(place.c, both[None], place.core(both)[None])


def normalize(values):
    center = values - jnp.mean(values, axis=-1, keepdims=True)
    inverse = lax.rsqrt(jnp.mean(center * center, axis=-1, keepdims=True) + EPS)
    return center * inverse, inverse


def norm_pull(grad, unit, inverse, gain):
    scaled = grad * gain
    return inverse * (
        scaled
        - jnp.mean(scaled, axis=-1, keepdims=True)
        - unit * jnp.mean(scaled * unit, axis=-1, keepdims=True)
    )


def dot(left, right, dims=((1,), (0,))):
    return lax.dot_general(left, right, (dims, ((), ())), preferred_element_type=F32)


NAMES = (
    "first_gain",
    "first_shift",
    "query_bias",
    "value_bias",
    "output_bias",
    "scale_one",
    "second_gain",
    "second_shift",
    "reduce_bias",
    "scale_two",
    "expand_bias",
)


def body(
    tokens,
    valid_mask,
    first_gain,
    first_shift,
    joint_weight,
    query_bias,
    value_bias,
    output_weight,
    output_bias,
    scale_one,
    second_gain,
    second_shift,
    expand_weight,
    expand_bias,
    reduce_weight,
    reduce_bias,
    scale_two,
    cotangent,
):
    shards = lax.axis_size("shard")
    place = Place(shards)
    c, y = place.c, place.y
    slab, width = joint_weight.shape[0], tokens.shape[2]
    local = tokens.shape[1]
    mine_rows = 2 * local
    hidden_width = expand_weight.shape[1]
    part = slab

    own_vectors = {
        "first_gain": first_gain,
        "first_shift": first_shift,
        "query_bias": query_bias,
        "value_bias": value_bias,
        "output_bias": output_bias,
        "scale_one": scale_one,
        "second_gain": second_gain,
        "second_shift": second_shift,
        "reduce_bias": reduce_bias,
        "scale_two": scale_two,
        "expand_bias": expand_bias,
    }
    packed = jnp.concatenate([own_vectors[name] for name in NAMES])[None]
    for bit in range(place.bits):
        packed = ordered(place.bit(bit), packed, place.swap(packed, 1 << bit))
    vectors = {}
    offset = 0
    for name in NAMES:
        size = own_vectors[name].shape[0]
        block = packed[:, offset : offset + size].astype(F32)
        offset += size
        if name == "expand_bias":
            block = pick(block.reshape(shards, 2, size // 2), c, 1)
        vectors[name] = block.reshape(-1)

    joint_piece = joint_weight.reshape(slab, 3, 2, 2, 2, 128).transpose(2, 3, 0, 4, 1, 5)
    joint_piece = pick(pick(joint_piece, c, 0), y, 0).reshape(slab, 768)
    out_piece = pick(pick(output_weight.reshape(slab, 2, 2, 2, 128), c, 1), y, 1)
    expand_own = pick(
        expand_weight.reshape(slab, shards, 2, hidden_width // (2 * shards)), c, 2
    ).reshape(slab, 2, 2, hidden_width // 8)
    expand_piece = pick(expand_own, y, 1)
    mixed_piece = jnp.concatenate([out_piece, expand_piece], axis=-1).reshape(slab, -1)
    reduce_piece = pick(pick(reduce_weight.reshape(2, 2, slab, width), c, 0), y, 0)

    def to_image(array):
        own, other = pick(array, y, 0), pick(array, 1 - y, 0)
        return jnp.concatenate([own, place.over_y(other)], axis=0)

    def from_image(array):
        own, other = array[:local], place.over_y(array[local:])
        return ordered(y, own[None], other[None])

    mine = to_image(tokens)
    joint_pieces = spread(place, joint_piece)
    both = jnp.concatenate([mine, place.core(mine)], axis=0)
    (joint_own,) = assemble(place, joint_pieces, [("columns", 0, 384)], "lay_joint")
    mixed_pieces = spread(place, mixed_piece)
    out_own, expand_full = assemble(
        place, mixed_pieces, [("columns", 0, 128), ("columns", 128, 512)], "lay_mixed"
    )
    reduce_pieces = spread(place, reduce_piece)
    (reduce_full,) = assemble(place, reduce_pieces, [("rows", 0, 512)], "lay_reduce")
    out_full = ordered(c, out_own, place.core(out_own), axis=1)
    back_mine = to_image(cotangent)
    back_both = jnp.concatenate([back_mine, place.core(back_mine)], axis=0)

    mask = pick(valid_mask, y, 0).reshape(4, local)
    mask = jnp.concatenate(
        [pick(mask, index, 0) for index in (2 * y + c, 2 - 2 * y + c, 2 * y + 1 - c, 3 - 2 * y - c)]
    )
    bias = jnp.where(mask > 0, 0.0, MASK_FILL).astype(F32)

    gain_one, shift_one = vectors["first_gain"], vectors["first_shift"]
    unit_both, _ = normalize(both.astype(F32))
    normed = (unit_both * gain_one + shift_one).astype(BF16)
    heads_of = lambda vector: pick(vector.reshape(2, 4, 128), c, 0)
    query_part, value_part = heads_of(vectors["query_bias"]), heads_of(vectors["value_bias"])
    joint_bias = jnp.stack([query_part, jnp.zeros_like(query_part), value_part], axis=1).reshape(-1)
    projected = (dot(normed, joint_own) + joint_bias).astype(BF16)
    attended, log_total = attention_forward(projected, bias[None, :])
    merged = ordered(c, attended[:mine_rows], place.core(attended[mine_rows:]), axis=1)
    mixed_out = dot(merged, out_full) + vectors["output_bias"]
    middle = mine.astype(F32) + vectors["scale_one"] * mixed_out
    unit_two, inverse_two = normalize(middle)
    second_normed = (unit_two * vectors["second_gain"] + vectors["second_shift"]).astype(BF16)

    second_both = jnp.concatenate([second_normed, place.core(second_normed)], axis=0)
    hidden = dot(second_both, expand_full) + vectors["expand_bias"]
    cumulative = 0.5 * (1.0 + lax.erf(hidden * 2**-0.5))
    active = (hidden * cumulative).astype(BF16)
    slope = (cumulative + hidden * (jnp.exp(-0.5 * hidden * hidden) * 0.3989422804014327)).astype(
        BF16
    )
    branch_parts = dot(active, reduce_full)
    branch = (
        branch_parts[:mine_rows]
        + place.core(branch_parts[mine_rows:].astype(BF16)).astype(F32)
        + vectors["reduce_bias"]
    )
    layer_out = from_image((middle + vectors["scale_two"] * branch).astype(BF16))

    grads = {}
    grad_out = back_mine.astype(F32)
    grads["scale_two"] = jnp.sum(grad_out * branch, axis=0)
    grad_branch = (back_both.astype(F32) * vectors["scale_two"]).astype(BF16)
    grads["reduce_bias"] = jnp.sum(grad_branch[:mine_rows].astype(F32), axis=0)
    grad_active = dot(grad_branch, reduce_full, ((1,), (1,)))
    grad_hidden = (grad_active * slope.astype(F32)).astype(BF16)
    grad_reduce = dot(active, grad_branch, ((0,), (0,)))
    expand_bias_grad = jnp.sum(grad_hidden.astype(F32), axis=0)
    grad_expand = dot(second_both, grad_hidden, ((0,), (0,)))
    second_parts = dot(grad_hidden, expand_full, ((1,), (1,)))
    grad_second = second_parts[:mine_rows] + place.core(
        second_parts[mine_rows:].astype(BF16)
    ).astype(F32)
    grads["second_gain"] = jnp.sum(grad_second * unit_two, axis=0)
    grads["second_shift"] = jnp.sum(grad_second, axis=0)
    grad_middle = grad_out + norm_pull(grad_second, unit_two, inverse_two, vectors["second_gain"])
    grads["scale_one"] = jnp.sum(grad_middle * mixed_out, axis=0)
    grad_mixed = (grad_middle * vectors["scale_one"]).astype(BF16)
    grads["output_bias"] = jnp.sum(grad_mixed.astype(F32), axis=0)
    grad_merged = dot(grad_mixed, out_full, ((1,), (1,))).astype(BF16)
    half = width // 2
    own_heads, other_heads = choose(c, (grad_merged[:, :half], grad_merged[:, half:]))
    grad_heads = jnp.concatenate([own_heads, place.core(other_heads)], axis=0)
    grad_output = dot(merged, grad_mixed, ((0,), (0,)))
    kept_output, sent_output = choose(c, (grad_output[:, :half], grad_output[:, half:]))
    grad_output = kept_output + place.core(sent_output.astype(BF16)).astype(F32)
    grad_projected = attention_backward(projected, grad_heads, log_total, bias[:, None])
    column_sums = jnp.sum(grad_projected.astype(F32), axis=0).reshape(4, 3, 128)
    grad_joint = dot(normed, grad_projected, ((0,), (0,)))
    first_parts = dot(grad_projected, joint_own, ((1,), (1,)))
    grad_first = first_parts[:mine_rows] + place.core(first_parts[mine_rows:].astype(BF16)).astype(
        F32
    )
    unit_one, inverse_one = normalize(mine.astype(F32))
    grads["first_gain"] = jnp.sum(grad_first * unit_one, axis=0)
    grads["first_shift"] = jnp.sum(grad_first, axis=0)
    tokens_grad = from_image(
        (grad_middle + norm_pull(grad_first, unit_one, inverse_one, gain_one)).astype(BF16)
    )

    outer = shards // 2
    quarter = hidden_width // 8

    def column_groups(value, size):
        groups = [
            value[:, k * size : (k + 1) * size].reshape(outer, 2, slab, size) for k in range(4)
        ]
        return groups[0::2], groups[1::2]

    def row_groups(value):
        value = value.reshape(outer, 2, 2, slab, width)
        halves = [
            [value[:, :, k, :, : width // 2], value[:, :, k, :, width // 2 :]] for k in range(2)
        ]
        return [half[0] for half in halves], [half[1] for half in halves]

    reduce_sum = collect(place, *row_groups(grad_reduce))
    beside = lambda left, right: [jnp.concatenate(p, axis=-1) for p in zip(left, right)]
    out_first, out_second = column_groups(grad_output, 128)
    expand_first, expand_second = column_groups(grad_expand, quarter)
    mixed_sum = collect(place, beside(out_first, expand_first), beside(out_second, expand_second))
    joint_sum = collect(place, *column_groups(grad_joint, 384))

    reduce_grad = share(place, reduce_sum).reshape(4 * slab, width).astype(F32)
    mixed_all = share(place, mixed_sum).reshape(2, 2, slab, 2, 128 + quarter)
    out_grad = mixed_all[..., :128].transpose(2, 0, 1, 3, 4).reshape(slab, width).astype(F32)
    expand_grad = mixed_all[..., 128:].transpose(0, 2, 1, 3, 4).reshape(2, slab, shards, -1)
    expand_grad = expand_grad.transpose(1, 2, 0, 3).reshape(slab, hidden_width).astype(F32)
    joint_grad = share(place, joint_sum).reshape(2, 2, slab, 2, 3, 128)
    joint_grad = joint_grad.transpose(2, 4, 0, 1, 3, 5).reshape(slab, 3 * width).astype(F32)

    def half_of(block, groups):
        zeros = jnp.zeros_like(block)
        return ordered(c, block[:, None], zeros[:, None], axis=1).reshape(groups, -1)

    grads["query_bias"] = half_of(column_sums[:, 0, :].reshape(1, -1), 1).reshape(-1)
    grads["value_bias"] = half_of(column_sums[:, 2, :].reshape(1, -1), 1).reshape(-1)
    grads["expand_bias"] = half_of(expand_bias_grad.reshape(shards, -1), shards).reshape(-1)
    totals = jnp.concatenate([grads[name].reshape(shards, -1) for name in NAMES], axis=1)
    for bit in range(place.bits - 1, -1, -1):
        totals = totals.reshape((2, -1) + totals.shape[1:])
        totals = pick(totals, place.bit(bit), 0) + place.swap(
            pick(totals, 1 - place.bit(bit), 0), 1 << bit
        )
    totals = totals.reshape(-1)
    totals = totals + place.over_y(totals)
    totals = totals + place.core(totals)
    shares = {}
    offset = 0
    for name in NAMES:
        size = own_vectors[name].shape[0]
        shares[name] = totals[offset : offset + size]
        offset += size

    return (
        layer_out,
        tokens_grad,
        shares["first_gain"],
        shares["first_shift"],
        joint_grad,
        shares["query_bias"],
        shares["value_bias"],
        out_grad,
        shares["output_bias"],
        shares["scale_one"],
        shares["second_gain"],
        shares["second_shift"],
        expand_grad,
        shares["expand_bias"],
        reduce_grad,
        shares["reduce_bias"],
        shares["scale_two"],
    )


def solution(mesh):
    row, rows = P("shard"), P("shard", None)
    image = P("shard", "seq", None)
    return jax.shard_map(
        body,
        mesh=mesh,
        in_specs=(
            image, rows, row, row, rows, row, row, rows, row, row, row, row, rows, row, rows, row, row, image,
        ),
        out_specs=(
            image, image, row, row, rows, row, row, rows, row, row, row, row, rows, row, rows, row, row,
        ),
        check_vma=False,
    )
```

```python
import functools

import jax
import jax.numpy as jnp
from jax import lax
from jax.experimental import pallas as pl
from jax.experimental.pallas import tpu as pltpu
from jax.sharding import PartitionSpec as P

HD = 64
EPS = 1e-06
MASK_FILL = -1e30
F32 = jnp.float32
BF16 = jnp.bfloat16
BOTH = ("shard", "seq")
VMEM_LIMIT = 60 * 1024 * 1024


def chunks_of(total, size):
    return [(start, min(size, total - start)) for start in range(0, total, size)]


def lane_half(shape, half):
    lanes = lax.broadcasted_iota(jnp.int32, shape, 1)
    return (lanes < HD) if half == 0 else (lanes >= HD)


def attention_forward_kernel(qkv_ref, bias_ref, out_ref, lse_ref):
    rows = qkv_ref.shape[0]
    keys = qkv_ref[:, 128:256]
    bias = bias_ref[...]
    zero = jnp.zeros((), BF16)
    values = [
        jnp.where(lane_half((rows, 128), half), qkv_ref[:, 256:384], zero) for half in range(2)
    ]
    for start, size in chunks_of(rows, 256):
        queries = qkv_ref[start : start + size, 0:128] * jnp.asarray(HD**-0.5, BF16)
        total = jnp.zeros((size, 128), F32)
        for half in range(2):
            own = jnp.where(lane_half((size, 128), half), queries, zero)
            scores = lax.dot_general(
                own, keys, (((1,), (1,)), ((), ())), preferred_element_type=F32
            )
            scores = scores + bias
            top = jnp.max(scores, axis=-1, keepdims=True)
            exponent = jnp.exp(scores - top)
            row_sum = jnp.sum(exponent, axis=-1, keepdims=True)
            part = jnp.dot(exponent.astype(BF16), values[half], preferred_element_type=F32)
            total = total + part * (1.0 / row_sum)
            log_total = top + jnp.log(row_sum)
            turned = jnp.transpose(jnp.broadcast_to(log_total, (size, 128)))
            lse_ref[0, half : half + 1, start : start + size] = turned[0:1, :]
        out_ref[start : start + size, :] = total.astype(BF16)


def attention_forward(qkv, bias_row, first, pairs):
    rows = qkv.shape[0]
    return pl.pallas_call(
        attention_forward_kernel,
        out_shape=(
            jax.ShapeDtypeStruct((rows, pairs * 128), BF16),
            jax.ShapeDtypeStruct((pairs, 8, rows), F32),
        ),
        grid=(pairs,),
        in_specs=[
            pl.BlockSpec((rows, 384), lambda p: (0, p + first)),
            pl.BlockSpec((1, rows), lambda p: (0, 0)),
        ],
        out_specs=(
            pl.BlockSpec((rows, 128), lambda p: (0, p)),
            pl.BlockSpec((1, 8, rows), lambda p: (p, 0, 0)),
        ),
        compiler_params=pltpu.CompilerParams(vmem_limit_bytes=VMEM_LIMIT),
        name="attend",
    )(qkv, bias_row)


def attention_backward_kernel(
    qkv_ref, grad_ref, lse_ref, bias_ref, out_ref, key_acc, value_acc
):
    rows = qkv_ref.shape[0]
    scale = jnp.asarray(HD**-0.5, BF16)
    zero = jnp.zeros((), BF16)
    keys = qkv_ref[:, 128:256]
    values = qkv_ref[:, 256:384]
    masked_keys = [jnp.where(lane_half((rows, 128), half), keys * scale, zero) for half in range(2)]
    bias = bias_ref[...]
    contract_lanes = (((1,), (1,)), ((), ()))
    for index, (start, size) in enumerate(chunks_of(rows, 256)):
        queries = qkv_ref[start : start + size, 0:128] * scale
        grads = grad_ref[start : start + size, :]
        grad_queries = jnp.zeros((size, 128), F32)
        key_part = jnp.zeros((rows, 128), F32)
        value_part = jnp.zeros((rows, 128), F32)
        for half in range(2):
            mask = lane_half((size, 128), half)
            own = jnp.where(mask, queries, zero)
            own_grads = jnp.where(mask, grads, zero)
            scores = lax.dot_general(keys, own, contract_lanes, preferred_element_type=F32)
            probs = jnp.exp(scores + bias - lse_ref[0, half : half + 1, start : start + size])
            grad_probs = lax.dot_general(
                values, own_grads, contract_lanes, preferred_element_type=F32
            )
            inner = jnp.sum(probs * grad_probs, axis=0, keepdims=True)
            grad_scores = (probs * (grad_probs - inner)).astype(BF16)
            value_part += jnp.dot(probs.astype(BF16), own_grads, preferred_element_type=F32)
            key_part += jnp.dot(grad_scores, own, preferred_element_type=F32)
            grad_queries += lax.dot_general(
                grad_scores, masked_keys[half], (((0,), (0,)), ((), ())), preferred_element_type=F32
            )
        if index == 0:
            key_acc[...] = key_part
            value_acc[...] = value_part
        else:
            key_acc[...] += key_part
            value_acc[...] += value_part
        out_ref[start : start + size, 0:128] = grad_queries.astype(BF16)
    out_ref[:, 128:256] = key_acc[...].astype(BF16)
    out_ref[:, 256:384] = value_acc[...].astype(BF16)


def attention_backward(qkv, grads, log_total, bias_column, first, pairs):
    rows = qkv.shape[0]
    return pl.pallas_call(
        attention_backward_kernel,
        out_shape=jax.ShapeDtypeStruct((rows, pairs * 384), BF16),
        grid=(pairs,),
        in_specs=[
            pl.BlockSpec((rows, 384), lambda p: (0, p + first)),
            pl.BlockSpec((rows, 128), lambda p: (0, p + first)),
            pl.BlockSpec((1, 8, rows), lambda p: (p, 0, 0)),
            pl.BlockSpec((rows, 1), lambda p: (0, 0)),
        ],
        out_specs=pl.BlockSpec((rows, 384), lambda p: (0, p)),
        scratch_shapes=[pltpu.VMEM((rows, 128), F32), pltpu.VMEM((rows, 128), F32)],
        compiler_params=pltpu.CompilerParams(vmem_limit_bytes=VMEM_LIMIT),
        name="attend_back",
    )(qkv, grads, log_total, bias_column)


class Place:
    def __init__(self, shards):
        self.shards = shards
        self.bits = shards.bit_length() - 1
        self.shard = lax.axis_index("shard")
        seq = lax.axis_index("seq")
        self.y = seq // 2
        self.c = seq % 2
        self.x = self.shard % 2

    def bit(self, index):
        return (self.shard // (1 << index)) % 2

    def swap(self, value, shard_flip=0, seq_flip=0):
        pairs = [
            (s * 4 + q, (s ^ shard_flip) * 4 + (q ^ seq_flip))
            for s in range(self.shards)
            for q in range(4)
        ]
        return lax.ppermute(value, BOTH, pairs)

    def core(self, value):
        return self.swap(value, 0, 1)

    def over_y(self, value):
        return self.swap(value, 0, 2)

    def over_x(self, value):
        return self.swap(value, 1, 0)


def ordered(first, own, other, axis=0):
    return jnp.where(
        first == 0,
        jnp.concatenate([own, other], axis=axis),
        jnp.concatenate([other, own], axis=axis),
    )


def pick(value, index, axis):
    return lax.dynamic_index_in_dim(value, index, axis, keepdims=False)


def bit_groups(bits):
    return [(low, min(2, bits - low)) for low in range(1, bits, 2)]


def after(value, *others):
    return lax.optimization_barrier((value,) + others)[0]


def gather_outer(place, piece):
    for low, count in bit_groups(place.bits):
        piece = jnp.concatenate(
            [piece] + [place.swap(piece, k << low) for k in range(1, 1 << count)], axis=0
        )
    return piece


def spread(place, held):
    half = held.shape[2] // 2
    first, second = held[:, :, :half], held[:, :, half:]
    first_x = place.over_x(first)
    second_y = place.over_y(second)
    return (
        (first, 0, 0, 0),
        (first_x, 1, 0, 0),
        (place.over_y(first), 0, 1, 0),
        (place.over_y(first_x), 1, 1, 0),
        (second, 0, 0, 1),
        (second_y, 0, 1, 1),
        (place.over_x(second), 1, 0, 1),
        (place.over_x(second_y), 1, 1, 1),
    )


def assemble_kernel(flips, plans, place_ref, *refs):
    count = len(flips)
    sources, outputs = refs[:count], refs[count:]
    x, y = place_ref[0], place_ref[1]
    for source, (flip_x, flip_y, half) in zip(sources, flips):
        to_x = lax.rem(x + flip_x, 2)
        to_y = lax.rem(y + flip_y, 2)
        for output, (kind, column, width) in zip(outputs, plans):
            value = source[0, :, column : column + width]
            if kind == "columns":
                at = pl.multiple_of(to_y * (2 * width) + half * width, 128)
                output[0, to_x, :, pl.ds(at, width)] = value
            else:
                output[0, to_x, to_y, :, half * width : (half + 1) * width] = value


def assemble(place, pieces, plans, name):
    arrays = [piece[0] for piece in pieces]
    flips = [piece[1:] for piece in pieces]
    outer, rows, columns = arrays[0].shape
    blocks = []
    for kind, _, width in plans:
        blocks.append((2, rows, 4 * width) if kind == "columns" else (2, 2, rows, 2 * width))

    def whole(block):
        zeros = (0,) * len(block)
        return pl.BlockSpec((1,) + block, lambda i, where: (i,) + zeros)

    def placed(block):
        zeros = (0,) * len(block)
        return pl.BlockSpec((1,) + block, lambda i, where: (where[2] ^ i,) + zeros)

    where = jnp.stack([place.x, place.y, place.shard // 2]).astype(jnp.int32)
    outputs = pl.pallas_call(
        functools.partial(assemble_kernel, flips, plans),
        out_shape=[jax.ShapeDtypeStruct((outer,) + block, BF16) for block in blocks],
        grid_spec=pltpu.PrefetchScalarGridSpec(
            num_scalar_prefetch=1,
            grid=(outer,),
            in_specs=[whole((rows, columns))] * len(arrays),
            out_specs=[placed(block) for block in blocks],
        ),
        name=name,
    )(where, *arrays)
    return [out.reshape(-1, out.shape[-1]) for out in outputs]


def step_down(value, axis, index, move):
    sent = pick(value, 1 - index, axis).astype(BF16)
    return pick(value, index, axis).astype(F32) + move(sent).astype(F32)


def choose(index, values):
    return jnp.where(index == 0, *values), jnp.where(index == 0, *values[::-1])


def collect_outer(place, held, kind):
    for low, count in bit_groups(place.bits)[::-1]:
        held = held.reshape((1 << count, -1) + held.shape[1:])
        own = (place.shard // (1 << low)) % (1 << count)
        total = pick(held, own, 0)
        for k in range(1, 1 << count):
            total = total + place.swap(pick(held, own ^ k, 0).astype(kind), k << low).astype(F32)
        held = total
    return held.reshape(held.shape[1:])


def collect(place, value):
    half = value.shape[-1] // 2
    first, second = value[..., :half], value[..., half:]
    first = step_down(first, 1, place.x, place.over_x)
    second = step_down(second, 2, place.y, place.over_y)
    first = step_down(first, 1, place.y, place.over_y)
    second = step_down(second, 1, place.x, place.over_x)
    return jnp.concatenate(
        [collect_outer(place, first, BF16), collect_outer(place, second, BF16)], axis=-1
    )


def share(place, piece):
    piece = piece.astype(BF16)
    both = ordered(place.y, piece, place.over_y(piece))
    return ordered(place.c, both[None], place.core(both)[None])


def normalize(values):
    center = values - jnp.mean(values, axis=-1, keepdims=True)
    inverse = lax.rsqrt(jnp.mean(center * center, axis=-1, keepdims=True) + EPS)
    return center * inverse, inverse


def norm_pull(grad, unit, inverse, gain):
    scaled = grad * gain
    return inverse * (
        scaled
        - jnp.mean(scaled, axis=-1, keepdims=True)
        - unit * jnp.mean(scaled * unit, axis=-1, keepdims=True)
    )


def dot(left, right, dims=((1,), (0,))):
    return lax.dot_general(left, right, (dims, ((), ())), preferred_element_type=F32)


NAMES = (
    "first_gain",
    "first_shift",
    "query_bias",
    "value_bias",
    "output_bias",
    "scale_one",
    "second_gain",
    "second_shift",
    "reduce_bias",
    "scale_two",
    "expand_bias",
)


def body(
    tokens,
    valid_mask,
    first_gain,
    first_shift,
    joint_weight,
    query_bias,
    value_bias,
    output_weight,
    output_bias,
    scale_one,
    second_gain,
    second_shift,
    expand_weight,
    expand_bias,
    reduce_weight,
    reduce_bias,
    scale_two,
    cotangent,
):
    shards = lax.axis_size("shard")
    place = Place(shards)
    c, y = place.c, place.y
    slab, width = joint_weight.shape[0], tokens.shape[2]
    local = tokens.shape[1]
    mine_rows = 2 * local
    hidden_width = expand_weight.shape[1]
    part = slab

    own_vectors = {
        "first_gain": first_gain,
        "first_shift": first_shift,
        "query_bias": query_bias,
        "value_bias": value_bias,
        "output_bias": output_bias,
        "scale_one": scale_one,
        "second_gain": second_gain,
        "second_shift": second_shift,
        "reduce_bias": reduce_bias,
        "scale_two": scale_two,
        "expand_bias": expand_bias,
    }
    packed = jnp.concatenate([own_vectors[name] for name in NAMES])[None]
    packed = ordered(place.x, packed, place.over_x(packed))
    outer = shards // 2
    relative = gather_outer(place, packed[None])
    packed = jnp.concatenate(
        [pick(relative, (place.shard // 2) ^ k, 0) for k in range(outer)], axis=0
    )
    vectors = {}
    offset = 0
    for name in NAMES:
        size = own_vectors[name].shape[0]
        block = packed[:, offset : offset + size].astype(F32)
        offset += size
        if name == "expand_bias":
            block = pick(block.reshape(shards, 2, size // 2), c, 1)
        vectors[name] = block.reshape(-1)

    joint_piece = joint_weight.reshape(slab, 3, 2, 2, 2, 128).transpose(2, 3, 0, 4, 1, 5)
    joint_piece = pick(pick(joint_piece, c, 0), y, 0).reshape(slab, 768)
    out_piece = pick(pick(output_weight.reshape(slab, 2, 2, 2, 128), c, 1), y, 1)
    expand_own = pick(
        expand_weight.reshape(slab, shards, 2, hidden_width // (2 * shards)), c, 2
    ).reshape(slab, 2, 2, hidden_width // 8)
    expand_piece = pick(expand_own, y, 1)
    mixed_piece = jnp.concatenate([out_piece, expand_piece], axis=-1).reshape(slab, -1)
    reduce_piece = pick(pick(reduce_weight.reshape(2, 2, slab, width), c, 0), y, 0)

    def to_image(array):
        own, other = pick(array, y, 0), pick(array, 1 - y, 0)
        return jnp.concatenate([own, place.over_y(other)], axis=0)

    def from_image(array):
        own, other = array[:local], place.over_y(array[local:])
        return ordered(y, own[None], other[None])

    mine = to_image(tokens)
    joint_held = gather_outer(place, joint_piece[None])
    both = jnp.concatenate([mine, place.core(mine)], axis=0)
    joint_pieces = spread(place, joint_held)
    (joint_own,) = assemble(place, joint_pieces, [("columns", 0, 384)], "lay_joint")
    mixed_held = gather_outer(place, after(mixed_piece[None], joint_held))
    joint_arrays = [piece[0] for piece in joint_pieces]
    mixed_pieces = spread(place, after(mixed_held, *joint_arrays))
    out_own, expand_full = assemble(
        place, mixed_pieces, [("columns", 0, 128), ("columns", 128, 512)], "lay_mixed"
    )
    reduce_held = gather_outer(place, after(reduce_piece[None], mixed_held))
    reduce_pieces = spread(place, reduce_held)
    (reduce_full,) = assemble(place, reduce_pieces, [("rows", 0, 512)], "lay_reduce")
    out_full = ordered(c, out_own, place.core(out_own), axis=1)
    back_mine = to_image(after(cotangent, out_own))
    back_both = jnp.concatenate([back_mine, place.core(back_mine)], axis=0)

    mask = pick(valid_mask, y, 0).reshape(4, local)
    mask = jnp.concatenate(
        [pick(mask, index, 0) for index in (2 * y + c, 2 - 2 * y + c, 2 * y + 1 - c, 3 - 2 * y - c)]
    )
    bias = jnp.where(mask > 0, 0.0, MASK_FILL).astype(F32)

    gain_one, shift_one = vectors["first_gain"], vectors["first_shift"]
    unit_both, _ = normalize(both.astype(F32))
    normed = (unit_both * gain_one + shift_one).astype(BF16)
    heads_of = lambda vector: pick(vector.reshape(2, 4, 128), c, 0)
    query_part, value_part = heads_of(vectors["query_bias"]), heads_of(vectors["value_bias"])
    joint_bias = jnp.stack([query_part, jnp.zeros_like(query_part), value_part], axis=1).reshape(-1)
    projected = (dot(normed, joint_own) + joint_bias).astype(BF16)
    attends = [attention_forward(projected, bias[None, :], first, 2) for first in (0, 2)]
    own_heads = jnp.concatenate([part[0][:mine_rows] for part in attends], axis=1)
    other_heads = jnp.concatenate([place.core(part[0][mine_rows:]) for part in attends], axis=1)
    merged = ordered(c, own_heads, other_heads, axis=1)
    mixed_out = dot(merged, out_full) + vectors["output_bias"]
    middle = mine.astype(F32) + vectors["scale_one"] * mixed_out
    unit_two, inverse_two = normalize(middle)
    second_normed = (unit_two * vectors["second_gain"] + vectors["second_shift"]).astype(BF16)

    second_both = jnp.concatenate([second_normed, place.core(second_normed)], axis=0)
    hidden = dot(second_both, expand_full) + vectors["expand_bias"]
    cumulative = 0.5 * (1.0 + lax.erf(hidden * 2**-0.5))
    active = (hidden * cumulative).astype(BF16)
    slope = (cumulative + hidden * (jnp.exp(-0.5 * hidden * hidden) * 0.3989422804014327)).astype(
        BF16
    )
    branch_parts = dot(active, reduce_full)
    branch = (
        branch_parts[:mine_rows]
        + place.core(branch_parts[mine_rows:].astype(BF16)).astype(F32)
        + vectors["reduce_bias"]
    )
    layer_out = from_image((middle + vectors["scale_two"] * branch).astype(BF16))

    grads = {}
    grad_out = back_mine.astype(F32)
    grads["scale_two"] = jnp.sum(grad_out * branch, axis=0)
    grad_branch = (back_both.astype(F32) * vectors["scale_two"]).astype(BF16)
    grads["reduce_bias"] = jnp.sum(grad_branch[:mine_rows].astype(F32), axis=0)
    grad_active = dot(grad_branch, reduce_full, ((1,), (1,)))
    grad_hidden = (grad_active * slope.astype(F32)).astype(BF16)
    grad_reduce = dot(active, grad_branch, ((0,), (0,)))
    expand_bias_grad = jnp.sum(grad_hidden.astype(F32), axis=0)
    grad_expand = dot(second_both, grad_hidden, ((0,), (0,)))
    second_parts = dot(grad_hidden, expand_full, ((1,), (1,)))
    grad_second = second_parts[:mine_rows] + place.core(
        second_parts[mine_rows:].astype(BF16)
    ).astype(F32)
    grads["second_gain"] = jnp.sum(grad_second * unit_two, axis=0)
    grads["second_shift"] = jnp.sum(grad_second, axis=0)
    grad_middle = grad_out + norm_pull(grad_second, unit_two, inverse_two, vectors["second_gain"])
    grads["scale_one"] = jnp.sum(grad_middle * mixed_out, axis=0)
    grad_mixed = (grad_middle * vectors["scale_one"]).astype(BF16)
    grads["output_bias"] = jnp.sum(grad_mixed.astype(F32), axis=0)
    grad_merged = dot(grad_mixed, out_full, ((1,), (1,))).astype(BF16)
    half = width // 2
    own_heads, other_heads = choose(c, (grad_merged[:, :half], grad_merged[:, half:]))
    grad_heads = jnp.concatenate([own_heads, place.core(other_heads)], axis=0)
    grad_output = dot(merged, grad_mixed, ((0,), (0,)))
    kept_output, sent_output = choose(c, (grad_output[:, :half], grad_output[:, half:]))
    grad_output = kept_output + place.core(sent_output.astype(BF16)).astype(F32)
    blocks = lambda value, rows: value.reshape(outer, 2, 2, rows, -1)
    column_sums, joint_grads, first_parts = [], [], 0.0
    for index, first in enumerate((0, 2)):
        part = attention_backward(projected, grad_heads, attends[index][1], bias[:, None], first, 2)
        column_sums.append(jnp.sum(part.astype(F32), axis=0).reshape(2, 3, 128))
        joint_grads.append(dot(normed, part, ((0,), (0,))))
        columns = joint_own[:, first * 384 : (first + 2) * 384]
        first_parts = first_parts + dot(part, columns, ((1,), (1,)))
    column_sums = jnp.concatenate(column_sums, axis=0)
    grad_first = first_parts[:mine_rows] + place.core(first_parts[mine_rows:].astype(BF16)).astype(
        F32
    )
    unit_one, inverse_one = normalize(mine.astype(F32))
    grads["first_gain"] = jnp.sum(grad_first * unit_one, axis=0)
    grads["first_shift"] = jnp.sum(grad_first, axis=0)
    tokens_grad = from_image(
        (grad_middle + norm_pull(grad_first, unit_one, inverse_one, gain_one)).astype(BF16)
    )

    half_slab = slab // 2
    reduce_sum = collect(place, blocks(grad_reduce, slab))
    expand_sum = collect(place, blocks(grad_expand, half_slab))
    out_sum = collect(place, blocks(grad_output, half_slab))
    joint_sums = [collect(place, blocks(value, half_slab)) for value in joint_grads]

    reduce_grad = share(place, reduce_sum).reshape(4 * slab, width).astype(F32)
    expand_grad = share(place, expand_sum).reshape(2, slab, shards, -1)
    expand_grad = expand_grad.transpose(1, 2, 0, 3).reshape(slab, hidden_width).astype(F32)
    out_grad = share(place, out_sum).transpose(1, 0, 2).reshape(slab, width).astype(F32)
    joint_grad = jnp.stack([share(place, value) for value in joint_sums], axis=1)
    joint_grad = joint_grad.reshape(2, 2, slab, 2, 3, 128)
    joint_grad = joint_grad.transpose(2, 4, 0, 1, 3, 5).reshape(slab, 3 * width).astype(F32)

    def half_of(block, groups):
        zeros = jnp.zeros_like(block)
        return ordered(c, block[:, None], zeros[:, None], axis=1).reshape(groups, -1)

    grads["query_bias"] = half_of(column_sums[:, 0, :].reshape(1, -1), 1).reshape(-1)
    grads["value_bias"] = half_of(column_sums[:, 2, :].reshape(1, -1), 1).reshape(-1)
    grads["expand_bias"] = half_of(expand_bias_grad.reshape(shards, -1), shards).reshape(-1)
    shares = {}
    late = ("first_gain", "first_shift", "query_bias", "value_bias")
    for names in ([name for name in NAMES if name not in late], late):
        totals = jnp.concatenate([grads[name].reshape(shards, -1) for name in names], axis=1)
        totals = totals.reshape(outer, 2, -1)
        totals = pick(totals, place.x, 1) + place.over_x(pick(totals, 1 - place.x, 1))
        totals = collect_outer(place, totals, F32)
        totals = totals + place.over_y(totals)
        totals = totals + place.core(totals)
        offset = 0
        for name in names:
            size = own_vectors[name].shape[0]
            shares[name] = totals[offset : offset + size]
            offset += size

    return (
        layer_out,
        tokens_grad,
        shares["first_gain"],
        shares["first_shift"],
        joint_grad,
        shares["query_bias"],
        shares["value_bias"],
        out_grad,
        shares["output_bias"],
        shares["scale_one"],
        shares["second_gain"],
        shares["second_shift"],
        expand_grad,
        shares["expand_bias"],
        reduce_grad,
        shares["reduce_bias"],
        shares["scale_two"],
    )


def solution(mesh):
    row, rows = P("shard"), P("shard", None)
    image = P("shard", "seq", None)
    return jax.shard_map(
        body,
        mesh=mesh,
        in_specs=(
            image, rows, row, row, rows, row, row, rows, row, row, row, row, rows, row, rows, row, row, image,
        ),
        out_specs=(
            image, image, row, row, rows, row, row, rows, row, row, row, row, rows, row, rows, row, row,
        ),
        check_vma=False,
    )
```

```python
import functools

import jax
import jax.numpy as jnp
from jax import lax
from jax.experimental import pallas as pl
from jax.experimental.pallas import tpu as pltpu
from jax.sharding import PartitionSpec as P


HD = 64
EPS = 1e-06
MASK_FILL = -1e30
F32 = jnp.float32
BF16 = jnp.bfloat16
BOTH = ("shard", "seq")
VMEM_LIMIT = 60 * 1024 * 1024


def chunks_of(total, size):
    return [(start, min(size, total - start)) for start in range(0, total, size)]


def lane_half(shape, half):
    lanes = lax.broadcasted_iota(jnp.int32, shape, 1)
    return (lanes < HD) if half == 0 else (lanes >= HD)


def attention_cost(rows, pairs, products):
    return pl.CostEstimate(
        flops=pairs * 2 * products * 2 * rows * rows * 128,
        bytes_accessed=pairs * rows * 128 * 2 * 4,
        transcendentals=pairs * 2 * rows * rows,
    )


def attention_forward_kernel(qkv_ref, bias_ref, out_ref, lse_ref):
    rows = qkv_ref.shape[0]
    keys = qkv_ref[:, 128:256]
    bias = bias_ref[...]
    zero = jnp.zeros((), BF16)
    values = [
        jnp.where(lane_half((rows, 128), half), qkv_ref[:, 256:384], zero) for half in range(2)
    ]
    for start, size in chunks_of(rows, 256):
        queries = qkv_ref[start : start + size, 0:128] * jnp.asarray(HD**-0.5, BF16)
        total = jnp.zeros((size, 128), F32)
        for half in range(2):
            own = jnp.where(lane_half((size, 128), half), queries, zero)
            scores = lax.dot_general(
                own, keys, (((1,), (1,)), ((), ())), preferred_element_type=F32
            )
            scores = scores + bias
            top = jnp.max(scores, axis=-1, keepdims=True)
            exponent = jnp.exp(scores - top)
            row_sum = jnp.sum(exponent, axis=-1, keepdims=True)
            part = jnp.dot(exponent.astype(BF16), values[half], preferred_element_type=F32)
            total = total + part * (1.0 / row_sum)
            log_total = top + jnp.log(row_sum)
            turned = jnp.transpose(jnp.broadcast_to(log_total, (size, 128)))
            lse_ref[0, half : half + 1, start : start + size] = turned[0:1, :]
        out_ref[start : start + size, :] = total.astype(BF16)


def attention_forward(qkv, bias_row, first, pairs):
    rows = qkv.shape[0]
    return pl.pallas_call(
        attention_forward_kernel,
        out_shape=(
            jax.ShapeDtypeStruct((rows, pairs * 128), BF16),
            jax.ShapeDtypeStruct((pairs, 8, rows), F32),
        ),
        grid=(pairs,),
        in_specs=[
            pl.BlockSpec((rows, 384), lambda p: (0, p + first)),
            pl.BlockSpec((1, rows), lambda p: (0, 0)),
        ],
        out_specs=(
            pl.BlockSpec((rows, 128), lambda p: (0, p)),
            pl.BlockSpec((1, 8, rows), lambda p: (p, 0, 0)),
        ),
        compiler_params=pltpu.CompilerParams(vmem_limit_bytes=VMEM_LIMIT),
        cost_estimate=attention_cost(rows, pairs, 2),
        name="attend",
    )(qkv, bias_row)


def attention_backward_kernel(
    qkv_ref, grad_ref, lse_ref, bias_ref, out_ref, key_acc, value_acc
):
    rows = qkv_ref.shape[0]
    scale = jnp.asarray(HD**-0.5, BF16)
    zero = jnp.zeros((), BF16)
    keys = qkv_ref[:, 128:256]
    values = qkv_ref[:, 256:384]
    masked_keys = [jnp.where(lane_half((rows, 128), half), keys * scale, zero) for half in range(2)]
    bias = bias_ref[...]
    contract_lanes = (((1,), (1,)), ((), ()))
    for index, (start, size) in enumerate(chunks_of(rows, 256)):
        queries = qkv_ref[start : start + size, 0:128] * scale
        grads = grad_ref[start : start + size, :]
        grad_queries = jnp.zeros((size, 128), F32)
        key_part = jnp.zeros((rows, 128), F32)
        value_part = jnp.zeros((rows, 128), F32)
        for half in range(2):
            mask = lane_half((size, 128), half)
            own = jnp.where(mask, queries, zero)
            own_grads = jnp.where(mask, grads, zero)
            scores = lax.dot_general(keys, own, contract_lanes, preferred_element_type=F32)
            probs = jnp.exp(scores + bias - lse_ref[0, half : half + 1, start : start + size])
            grad_probs = lax.dot_general(
                values, own_grads, contract_lanes, preferred_element_type=F32
            )
            inner = jnp.sum(probs * grad_probs, axis=0, keepdims=True)
            grad_scores = (probs * (grad_probs - inner)).astype(BF16)
            value_part += jnp.dot(probs.astype(BF16), own_grads, preferred_element_type=F32)
            key_part += jnp.dot(grad_scores, own, preferred_element_type=F32)
            grad_queries += lax.dot_general(
                grad_scores, masked_keys[half], (((0,), (0,)), ((), ())), preferred_element_type=F32
            )
        if index == 0:
            key_acc[...] = key_part
            value_acc[...] = value_part
        else:
            key_acc[...] += key_part
            value_acc[...] += value_part
        out_ref[start : start + size, 0:128] = grad_queries.astype(BF16)
    out_ref[:, 128:256] = key_acc[...].astype(BF16)
    out_ref[:, 256:384] = value_acc[...].astype(BF16)


def attention_backward(qkv, grads, log_total, bias_column, first, pairs):
    rows = qkv.shape[0]
    return pl.pallas_call(
        attention_backward_kernel,
        out_shape=jax.ShapeDtypeStruct((rows, pairs * 384), BF16),
        grid=(pairs,),
        in_specs=[
            pl.BlockSpec((rows, 384), lambda p: (0, p + first)),
            pl.BlockSpec((rows, 128), lambda p: (0, p + first)),
            pl.BlockSpec((1, 8, rows), lambda p: (p, 0, 0)),
            pl.BlockSpec((rows, 1), lambda p: (0, 0)),
        ],
        out_specs=pl.BlockSpec((rows, 384), lambda p: (0, p)),
        scratch_shapes=[pltpu.VMEM((rows, 128), F32), pltpu.VMEM((rows, 128), F32)],
        compiler_params=pltpu.CompilerParams(vmem_limit_bytes=VMEM_LIMIT),
        cost_estimate=attention_cost(rows, pairs, 5),
        name="attend_back",
    )(qkv, grads, log_total, bias_column)


class Place:
    def __init__(self, shards):
        self.shards = shards
        self.bits = shards.bit_length() - 1
        self.shard = lax.axis_index("shard")
        seq = lax.axis_index("seq")
        self.y = seq // 2
        self.c = seq % 2
        self.x = self.shard % 2

    def bit(self, index):
        return (self.shard // (1 << index)) % 2

    def swap(self, value, shard_flip=0, seq_flip=0):
        pairs = [
            (s * 4 + q, (s ^ shard_flip) * 4 + (q ^ seq_flip))
            for s in range(self.shards)
            for q in range(4)
        ]
        return lax.ppermute(value, BOTH, pairs)

    def core(self, value):
        return self.swap(value, 0, 1)

    def over_y(self, value):
        return self.swap(value, 0, 2)

    def over_x(self, value):
        return self.swap(value, 1, 0)


def ordered(first, own, other, axis=0):
    return jnp.where(
        first == 0,
        jnp.concatenate([own, other], axis=axis),
        jnp.concatenate([other, own], axis=axis),
    )


def pick(value, index, axis):
    return lax.dynamic_index_in_dim(value, index, axis, keepdims=False)


def bit_groups(bits):
    return [(low, min(2, bits - low)) for low in range(1, bits, 2)]


def after(value, *others):
    return lax.optimization_barrier((value,) + others)[0]


def gather_outer(place, piece, *late):
    for low, count in bit_groups(place.bits):
        moved = [place.swap(piece, k << low) for k in range(1, 1 << count)]
        piece = jnp.concatenate([piece] + [after(value, *late) for value in moved], axis=0)
    return piece


def spread(place, held, late_one=(), late_two=()):
    half = held.shape[2] // 2
    first, second = held[:, :, :half], held[:, :, half:]
    first_x = after(place.over_x(first), *late_one)
    second_y = after(place.over_y(second), *late_one)
    first_y = after(place.over_y(first), *late_one)
    second_x = after(place.over_x(second), *late_one)
    first_xy = after(place.over_y(first_x), *late_two)
    second_xy = after(place.over_x(second_y), *late_two)
    return (
        (first, 0, 0, 0),
        (first_x, 1, 0, 0),
        (first_y, 0, 1, 0),
        (first_xy, 1, 1, 0),
        (second, 0, 0, 1),
        (second_y, 0, 1, 1),
        (second_x, 1, 0, 1),
        (second_xy, 1, 1, 1),
    )


def assemble_kernel(flips, plans, place_ref, *refs):
    count = len(flips)
    sources, outputs = refs[:count], refs[count:]
    x, y = place_ref[0], place_ref[1]
    for source, (flip_x, flip_y, half) in zip(sources, flips):
        to_x = lax.rem(x + flip_x, 2)
        to_y = lax.rem(y + flip_y, 2)
        for output, (kind, column, width) in zip(outputs, plans):
            value = source[0, :, column : column + width]
            if kind == "columns":
                at = pl.multiple_of(to_y * (2 * width) + half * width, 128)
                output[0, to_x, :, pl.ds(at, width)] = value
            else:
                output[0, to_x, to_y, :, half * width : (half + 1) * width] = value


def assemble(place, pieces, plans):
    arrays = [piece[0] for piece in pieces]
    flips = [piece[1:] for piece in pieces]
    outer, rows, columns = arrays[0].shape
    blocks = []
    for kind, _, width in plans:
        blocks.append((2, rows, 4 * width) if kind == "columns" else (2, 2, rows, 2 * width))

    def whole(block):
        zeros = (0,) * len(block)
        return pl.BlockSpec((1,) + block, lambda i, where: (i,) + zeros)

    def placed(block):
        zeros = (0,) * len(block)
        return pl.BlockSpec((1,) + block, lambda i, where: (where[2] ^ i,) + zeros)

    where = jnp.stack([place.x, place.y, place.shard // 2]).astype(jnp.int32)
    outputs = pl.pallas_call(
        functools.partial(assemble_kernel, flips, plans),
        out_shape=[jax.ShapeDtypeStruct((outer,) + block, BF16) for block in blocks],
        grid_spec=pltpu.PrefetchScalarGridSpec(
            num_scalar_prefetch=1,
            grid=(outer,),
            in_specs=[whole((rows, columns))] * len(arrays),
            out_specs=[placed(block) for block in blocks],
        ),
    )(where, *arrays)
    return [out.reshape(-1, out.shape[-1]) for out in outputs]


def step_down(value, axis, index, move, late=()):
    sent = pick(value, 1 - index, axis).astype(BF16)
    return pick(value, index, axis).astype(F32) + after(move(sent), *late).astype(F32)


def choose(index, values):
    return jnp.where(index == 0, *values), jnp.where(index == 0, *values[::-1])


def collect_outer(place, held, kind, late=()):
    for low, count in bit_groups(place.bits)[::-1]:
        held = held.reshape((1 << count, -1) + held.shape[1:])
        own = (place.shard // (1 << low)) % (1 << count)
        total = pick(held, own, 0)
        for k in range(1, 1 << count):
            moved = place.swap(pick(held, own ^ k, 0).astype(kind), k << low)
            total = total + after(moved, *late).astype(F32)
        held = total
    return held.reshape(held.shape[1:])


def collect_one(place, first, second, late=()):
    return (
        step_down(first, 1, place.x, place.over_x, late),
        step_down(second, 2, place.y, place.over_y, late),
    )


def collect_two(place, first, second, late=()):
    return (
        step_down(first, 1, place.y, place.over_y, late),
        step_down(second, 1, place.x, place.over_x, late),
    )


def collect_last(place, first, second, late=()):
    return collect_outer(place, jnp.concatenate([first, second], axis=-1), BF16, late)


def share(place, piece, late=()):
    piece = piece.astype(BF16)
    both = jnp.concatenate([piece, after(place.over_y(piece), *late)], axis=0)
    return both, place.core(both)


def finish_kernel(moves, row_core, place_ref, own_ref, other_ref, out_ref):
    y, c = place_ref[0], place_ref[1]
    rows = own_ref.shape[0] // 2
    for ref, core in ((own_ref, c), (other_ref, 1 - c)):
        for half, row_y in ((0, y), (1, 1 - y)):
            to_row = pl.multiple_of(core * row_core + row_y * rows, 8)
            for column, width, target, step in moves:
                value = ref[half * rows : (half + 1) * rows, column : column + width]
                if step:
                    target = pl.multiple_of(target + core * step, 128)
                out_ref[pl.ds(to_row, rows), pl.ds(target, width)] = value.astype(F32)


def finish(place, pairs, moves, shape, row_core):
    own = jnp.concatenate([pair[0] for pair in pairs], axis=1) if len(pairs) > 1 else pairs[0][0]
    other = jnp.concatenate([pair[1] for pair in pairs], axis=1) if len(pairs) > 1 else pairs[0][1]
    block = lambda size: pl.BlockSpec(size, lambda i, where: (0, 0))
    return pl.pallas_call(
        functools.partial(finish_kernel, moves, row_core),
        out_shape=jax.ShapeDtypeStruct(shape, F32),
        grid_spec=pltpu.PrefetchScalarGridSpec(
            num_scalar_prefetch=1,
            grid=(1,),
            in_specs=[block(own.shape), block(other.shape)],
            out_specs=block(shape),
        ),
        compiler_params=pltpu.CompilerParams(vmem_limit_bytes=VMEM_LIMIT),
    )(jnp.stack([place.y, place.c]).astype(jnp.int32), own, other)


def normalize(values):
    center = values - jnp.mean(values, axis=-1, keepdims=True)
    inverse = lax.rsqrt(jnp.mean(center * center, axis=-1, keepdims=True) + EPS)
    return center * inverse, inverse


def norm_pull(grad, unit, inverse, gain):
    scaled = grad * gain
    return inverse * (
        scaled
        - jnp.mean(scaled, axis=-1, keepdims=True)
        - unit * jnp.mean(scaled * unit, axis=-1, keepdims=True)
    )


def dot(left, right, dims=((1,), (0,))):
    return lax.dot_general(left, right, (dims, ((), ())), preferred_element_type=F32)


NAMES = (
    "first_gain",
    "first_shift",
    "query_bias",
    "value_bias",
    "output_bias",
    "scale_one",
    "second_gain",
    "second_shift",
    "reduce_bias",
    "scale_two",
    "expand_bias",
)


def body(
    tokens,
    valid_mask,
    first_gain,
    first_shift,
    joint_weight,
    query_bias,
    value_bias,
    output_weight,
    output_bias,
    scale_one,
    second_gain,
    second_shift,
    expand_weight,
    expand_bias,
    reduce_weight,
    reduce_bias,
    scale_two,
    cotangent,
):
    shards = lax.axis_size("shard")
    place = Place(shards)
    c, y = place.c, place.y
    slab, width = joint_weight.shape[0], tokens.shape[2]
    local = tokens.shape[1]
    mine_rows = 2 * local
    hidden_width = expand_weight.shape[1]
    part = slab

    own_vectors = {
        "first_gain": first_gain,
        "first_shift": first_shift,
        "query_bias": query_bias,
        "value_bias": value_bias,
        "output_bias": output_bias,
        "scale_one": scale_one,
        "second_gain": second_gain,
        "second_shift": second_shift,
        "reduce_bias": reduce_bias,
        "scale_two": scale_two,
        "expand_bias": expand_bias,
    }
    packed = jnp.concatenate([own_vectors[name] for name in NAMES])[None]
    packed = ordered(place.x, packed, place.over_x(packed))
    outer = shards // 2
    relative = gather_outer(place, packed[None])
    packed = jnp.concatenate(
        [pick(relative, (place.shard // 2) ^ k, 0) for k in range(outer)], axis=0
    )
    vectors = {}
    offset = 0
    for name in NAMES:
        size = own_vectors[name].shape[0]
        block = packed[:, offset : offset + size].astype(F32)
        offset += size
        if name == "expand_bias":
            block = pick(block.reshape(shards, 2, size // 2), c, 1)
        vectors[name] = block.reshape(-1)

    joint_piece = joint_weight.reshape(slab, 3, 2, 2, 2, 128).transpose(2, 3, 0, 4, 1, 5)
    joint_piece = pick(pick(joint_piece, c, 0), y, 0).reshape(slab, 768)
    out_piece = pick(pick(output_weight.reshape(slab, 2, 2, 2, 128), c, 1), y, 1)
    expand_own = pick(
        expand_weight.reshape(slab, shards, 2, hidden_width // (2 * shards)), c, 2
    ).reshape(slab, 2, 2, hidden_width // 8)
    expand_piece = pick(expand_own, y, 1)
    mixed_piece = jnp.concatenate([out_piece, expand_piece], axis=-1).reshape(slab, -1)
    reduce_piece = pick(pick(reduce_weight.reshape(2, 2, slab, width), c, 0), y, 0)

    def to_image(array):
        own, other = pick(array, y, 0), pick(array, 1 - y, 0)
        return jnp.concatenate([own, place.over_y(other)], axis=0)

    def from_image(array):
        own, other = array[:local], place.over_y(array[local:])
        return ordered(y, own[None], other[None])

    mine = to_image(tokens)
    joint_held = gather_outer(place, joint_piece[None])
    both = jnp.concatenate([mine, place.core(mine)], axis=0)
    joint_pieces = spread(place, joint_held)
    (joint_own,) = assemble(place, joint_pieces, [("columns", 0, 384)])
    back_mine = to_image(cotangent)
    back_both = jnp.concatenate([back_mine, place.core(back_mine)], axis=0)

    mask = pick(valid_mask, y, 0).reshape(4, local)
    mask = jnp.concatenate(
        [pick(mask, index, 0) for index in (2 * y + c, 2 - 2 * y + c, 2 * y + 1 - c, 3 - 2 * y - c)]
    )
    bias = jnp.where(mask > 0, 0.0, MASK_FILL).astype(F32)

    gain_one, shift_one = vectors["first_gain"], vectors["first_shift"]
    unit_both, _ = normalize(both.astype(F32))
    normed = (unit_both * gain_one + shift_one).astype(BF16)
    heads_of = lambda vector: pick(vector.reshape(2, 4, 128), c, 0)
    query_part, value_part = heads_of(vectors["query_bias"]), heads_of(vectors["value_bias"])
    joint_bias = jnp.stack([query_part, jnp.zeros_like(query_part), value_part], axis=1).reshape(-1)
    projected = (dot(normed, joint_own) + joint_bias).astype(BF16)
    attends = [attention_forward(projected, bias[None, :], 0, 2)]

    mixed_held = gather_outer(place, after(mixed_piece[None], joint_held))
    joint_arrays = [piece[0] for piece in joint_pieces]
    mixed_pieces = spread(place, after(mixed_held, *joint_arrays), (projected,), (attends[0][0],))
    reduce_held = gather_outer(place, after(reduce_piece[None], mixed_held), projected)
    mixed_arrays = [piece[0] for piece in mixed_pieces]
    attends.append(
        attention_forward(after(projected, reduce_held, *mixed_arrays), bias[None, :], 2, 2)
    )
    out_own, expand_full = assemble(
        place, mixed_pieces, [("columns", 0, 128), ("columns", 128, 512)]
    )
    reduce_pieces = spread(place, reduce_held, (attends[1][0],))
    (reduce_full,) = assemble(place, reduce_pieces, [("rows", 0, 512)])
    out_full = ordered(c, out_own, place.core(out_own), axis=1)
    own_heads = jnp.concatenate([part[0][:mine_rows] for part in attends], axis=1)
    other_heads = jnp.concatenate([place.core(part[0][mine_rows:]) for part in attends], axis=1)
    merged = ordered(c, own_heads, other_heads, axis=1)
    mixed_out = dot(merged, out_full) + vectors["output_bias"]
    middle = mine.astype(F32) + vectors["scale_one"] * mixed_out
    unit_two, inverse_two = normalize(middle)
    second_normed = (unit_two * vectors["second_gain"] + vectors["second_shift"]).astype(BF16)

    second_both = jnp.concatenate([second_normed, place.core(second_normed)], axis=0)
    hidden = dot(second_both, expand_full) + vectors["expand_bias"]
    cumulative = 0.5 * (1.0 + lax.erf(hidden * 2**-0.5))
    active = (hidden * cumulative).astype(BF16)
    slope = (cumulative + hidden * (jnp.exp(-0.5 * hidden * hidden) * 0.3989422804014327)).astype(
        BF16
    )
    grad_branch = (back_both.astype(F32) * vectors["scale_two"]).astype(BF16)
    cut = lambda value: (value[:, : value.shape[1] // 2], value[:, value.shape[1] // 2 :])
    reduce_grads = [dot(active, value, ((0,), (0,))) for value in cut(grad_branch)]
    branch_parts = dot(after(active, *reduce_grads), reduce_full)
    branch = (
        branch_parts[:mine_rows]
        + place.core(branch_parts[mine_rows:].astype(BF16)).astype(F32)
        + vectors["reduce_bias"]
    )
    layer_out = from_image((middle + vectors["scale_two"] * branch).astype(BF16))

    grads = {}
    grad_out = back_mine.astype(F32)
    grads["scale_two"] = jnp.sum(grad_out * branch, axis=0)
    grads["reduce_bias"] = jnp.sum(grad_branch[:mine_rows].astype(F32), axis=0)
    grad_active = dot(after(grad_branch, branch_parts), reduce_full, ((1,), (1,)))
    grad_hidden = (grad_active * slope.astype(F32)).astype(BF16)
    expand_bias_grad = jnp.sum(grad_hidden.astype(F32), axis=0)
    half_slab = slab // 2
    blocks = lambda value, rows: value.reshape(outer, 2, 2, rows, -1)
    reduce_sums = collect_one(
        place, *[blocks(value, slab) for value in reduce_grads], (grad_hidden,)
    )
    second_parts = dot(after(grad_hidden, *reduce_sums), expand_full, ((1,), (1,)))
    expand_grads = [
        dot(second_both, value, ((0,), (0,))) for value in cut(after(grad_hidden, second_parts))
    ]
    grad_second = second_parts[:mine_rows] + place.core(
        second_parts[mine_rows:].astype(BF16)
    ).astype(F32)
    grads["second_gain"] = jnp.sum(grad_second * unit_two, axis=0)
    grads["second_shift"] = jnp.sum(grad_second, axis=0)
    grad_middle = grad_out + norm_pull(grad_second, unit_two, inverse_two, vectors["second_gain"])
    grads["scale_one"] = jnp.sum(grad_middle * mixed_out, axis=0)
    grad_mixed = (grad_middle * vectors["scale_one"]).astype(BF16)
    grads["output_bias"] = jnp.sum(grad_mixed.astype(F32), axis=0)
    grad_merged = dot(grad_mixed, out_full, ((1,), (1,))).astype(BF16)
    half = width // 2
    own_heads, other_heads = choose(c, (grad_merged[:, :half], grad_merged[:, half:]))
    grad_heads = jnp.concatenate([own_heads, place.core(other_heads)], axis=0)
    grad_output = dot(merged, grad_mixed, ((0,), (0,)))
    kept_output, sent_output = choose(c, (grad_output[:, :half], grad_output[:, half:]))
    grad_output = kept_output + place.core(sent_output.astype(BF16)).astype(F32)
    reduce_sums = collect_two(place, *reduce_sums, tuple(expand_grads))
    expand_sums = collect_one(
        place, *[blocks(value, half_slab) for value in expand_grads], (grad_merged,)
    )
    grad_heads = after(grad_heads, *reduce_sums, *expand_sums)
    column_sums, joint_grads, parts, first_parts = [], [], [], 0.0
    for index, first in enumerate((0, 2)):
        log_total = attends[index][1]
        part = attention_backward(projected, grad_heads, log_total, bias[:, None], first, 2)
        parts.append(part)
        joint_grads.append([dot(normed, value, ((0,), (0,))) for value in cut(part)])
        part = after(part, *joint_grads[-1])
        if index == 0:
            reduce_sum = collect_last(place, *reduce_sums, (parts[0],))
            expand_sums = collect_two(place, *expand_sums, (parts[0],))
            grad_heads = after(grad_heads, part, reduce_sum, *expand_sums)
        column_sums.append(jnp.sum(part.astype(F32), axis=0).reshape(2, 3, 128))
        columns = joint_own[:, first * 384 : (first + 2) * 384]
        first_parts = first_parts + dot(part, columns, ((1,), (1,)))
    column_sums = jnp.concatenate(column_sums, axis=0)
    grad_first = first_parts[:mine_rows] + place.core(first_parts[mine_rows:].astype(BF16)).astype(
        F32
    )
    unit_one, inverse_one = normalize(mine.astype(F32))
    grads["first_gain"] = jnp.sum(grad_first * unit_one, axis=0)
    grads["first_shift"] = jnp.sum(grad_first, axis=0)
    tokens_local = (grad_middle + norm_pull(grad_first, unit_one, inverse_one, gain_one)).astype(BF16)
    tokens_grad = from_image(tokens_local)

    def summed(pair, late_one=(), late_two=()):
        value = collect_one(place, *[blocks(value, half_slab) for value in pair], late_one)
        value = collect_two(place, *value, late_two)
        return share(place, collect_last(place, *value))

    reduce_pair = share(place, reduce_sum, (parts[1],))
    expand_sum = collect_last(place, *expand_sums, (parts[1],))
    expand_pair = share(place, expand_sum)
    joint_first = [jnp.concatenate(p, axis=1) for p in zip(cut(grad_output), joint_grads[0])]
    out_pair = summed(joint_first, (parts[1],))
    joint_pair = summed(joint_grads[1], (first_parts,), (tokens_local,))
    per_shard = hidden_width // (2 * shards)
    reduce_grad = finish(place, [reduce_pair], [(0, width, 0, 0)], (4 * slab, width), 2 * slab)
    expand_grad = finish(
        place,
        [expand_pair],
        [(k * per_shard, per_shard, 2 * k * per_shard, per_shard) for k in range(shards)],
        (slab, hidden_width),
        0,
    )
    eighth = width // 8
    with_out = (eighth * 2 + 384) * 2
    half = with_out // 2
    out_grad = finish(
        place,
        [out_pair],
        [
            (0, eighth * 2, 0, width // 2),
            (half, eighth * 2, eighth * 2, width // 2),
        ],
        (slab, width),
        0,
    )
    starts = (eighth * 2, half + eighth * 2, with_out, with_out + 384)
    joint_grad = finish(
        place,
        [out_pair, joint_pair],
        [
            (starts[pair] + kind * 128, 128, kind * width + pair * 128, width // 2)
            for pair in range(4)
            for kind in range(3)
        ],
        (slab, 3 * width),
        0,
    )

    def half_of(block, groups):
        zeros = jnp.zeros_like(block)
        return ordered(c, block[:, None], zeros[:, None], axis=1).reshape(groups, -1)

    grads["query_bias"] = half_of(column_sums[:, 0, :].reshape(1, -1), 1).reshape(-1)
    grads["value_bias"] = half_of(column_sums[:, 2, :].reshape(1, -1), 1).reshape(-1)
    grads["expand_bias"] = half_of(expand_bias_grad.reshape(shards, -1), shards).reshape(-1)
    shares = {}
    for names in (NAMES,):
        totals = jnp.concatenate([grads[name].reshape(shards, -1) for name in names], axis=1)
        totals = totals.reshape(outer, 2, -1)
        totals = pick(totals, place.x, 1) + place.over_x(pick(totals, 1 - place.x, 1))
        totals = collect_outer(place, totals, F32)
        totals = totals + place.over_y(totals)
        totals = totals + place.core(totals)
        offset = 0
        for name in names:
            size = own_vectors[name].shape[0]
            shares[name] = totals[offset : offset + size]
            offset += size

    return (
        layer_out,
        tokens_grad,
        shares["first_gain"],
        shares["first_shift"],
        joint_grad,
        shares["query_bias"],
        shares["value_bias"],
        out_grad,
        shares["output_bias"],
        shares["scale_one"],
        shares["second_gain"],
        shares["second_shift"],
        expand_grad,
        shares["expand_bias"],
        reduce_grad,
        shares["reduce_bias"],
        shares["scale_two"],
    )


def solution(mesh):
    row, rows = P("shard"), P("shard", None)
    image = P("shard", "seq", None)
    return jax.shard_map(
        body,
        mesh=mesh,
        in_specs=(
            image, rows, row, row, rows, row, row, rows, row, row, row, row, rows, row, rows, row, row, image,
        ),
        out_specs=(
            image, image, row, row, rows, row, row, rows, row, row, row, row, rows, row, rows, row, row,
        ),
        check_vma=False,
    )
```
